256 devices in a mesh: tiles: 64 (over y, z, core), rep: 4 (over x).
Axes of the slice: x: 4, y: 4, z: 8, core: 2. Of those that a mesh axis runs over, the one named last changes fastest.
Arguments:
- trailing_tiles: float32 [5120, 256, 256], P(('tiles', 'rep')), may hold values from -6 to 6
- panel_rows: float32 [128, 256, 512], P('tiles'), may hold values from -3 to 3
- pivot_blocks: float32 [2, 256, 256], replicated
- coupling: float32 [256, 256], replicated, may hold values from -0.1875 to 0.1875
- row_ids: int32 [128], replicated, may hold values from 2 to 96, as said below
- membership: int32 [64, 24], replicated, may hold values from 2 to 96, as said below
- tile_pairs: int32 [5120, 2], P(('tiles', 'rep')), may hold values from 0 to 24, as said below
Outputs:
- updated_tiles: float32 [5120, 256, 256], P(('tiles', 'rep'))
- factors: float32 [128, 256, 512], P('tiles')
- pivot_diag: float32 [2, 256], replicated
The draws below stay inside these ranges and needn't reach their ends.
Inputs may be any that keep to these rules, and one draw needn't show every extreme that they name: `row_ids`: each row block 2 to 95 stands in exactly one slot; the other slots hold 96. `membership`: entries are row blocks 2 to 95, or 96 for none. `tile_pairs`: a slot's first entry is below 12, its second from 12 to 23, or both are 24 for an empty slot; over all devices every unordered pair of row blocks 2 to 96 - 1 (a block with itself too) is listed exactly once; some device fills all 20 slots.
All inputs are finite; a program needn't handle non-finite values.
Results may differ from the reference program's by a relative error of at most 0.00005.
Values sent between devices are 32-bit elements; how exact they have to be, the bound alone decides.
No kernel may reach another device: no remote copies, remote signals or barrier semaphores. Data moves between devices by JAX's collectives and lax.ppermute only.
A program may use at most 128 MiB of HBM per device.

```python
import math
import jax
import jax.numpy as jnp
from jax import lax

B = 256
NB = 96
GRIDP = 8
NT = 94
GQ = 8
KB = 12
KQ = 12
NEEDG = 24
RPD = 2
SLOTS = 20
N_TILES = 64
N_REP = 4


def layout_tables(key):
    layout_key = jax.random.fold_in(key, 7)
    perm_key, order_key, turn_key = jax.random.split(layout_key, 3)
    labels = jax.random.permutation(perm_key, NT) + 2
    padded = jnp.concatenate([labels, jnp.full((1,), NB)]).astype(jnp.int32)
    groups = jnp.arange(N_TILES)
    row_class = groups // GQ
    col_class = groups % GQ
    upper_label = jnp.arange(KB)[None, :] * GRIDP + row_class[:, None]
    lower_label = jnp.arange(KQ)[None, :] * GQ + col_class[:, None]
    row_part = padded[jnp.minimum(upper_label, NT)]
    col_part = padded[jnp.minimum(lower_label, NT)]
    membership = jnp.concatenate([row_part, col_part], axis=1).astype(jnp.int32)
    usable = (upper_label[:, :, None] < NT) & (lower_label[:, None, :] <= upper_label[:, :, None])
    usable = usable.reshape(N_TILES, KB * KQ)
    scores = jax.random.randint(order_key, (N_TILES, KB * KQ), 0, 65536) * (KB * KQ) + jnp.arange(KB * KQ)[None, :]
    ordering = jnp.argsort(scores, axis=1)
    picked = jnp.take_along_axis(usable, ordering, axis=1)
    ranking = jnp.cumsum(picked.astype(jnp.int32), axis=1) - 1
    offset = jax.random.randint(turn_key, (N_TILES, 1), 0, N_REP)
    replica = (ranking + offset) % N_REP
    spare_slot = N_TILES * N_REP * SLOTS
    target = (groups[:, None] * N_REP + replica) * SLOTS + ranking // N_REP
    target = jnp.where(picked, target, spare_slot)
    entries = jnp.stack([ordering // KQ, KB + ordering % KQ], axis=-1).astype(jnp.int32)
    pair_table = jnp.full((spare_slot + 1, 2), NEEDG, jnp.int32).at[target.reshape(-1)].set(entries.reshape(-1, 2))
    return (membership, pair_table[:spare_slot])


def draw_membership(key, part):
    return layout_tables(key)[0]


def draw_tile_pairs(key, part):
    return layout_tables(key)[1]


def draw_row_ids(key, part):
    shuffle = jax.random.permutation(jax.random.fold_in(key, 11), N_TILES * RPD)
    return jnp.where(shuffle < NT, shuffle + 2, NB).astype(jnp.int32)


def draw_pivot_blocks(key, part):
    noise_key, diag_key = jax.random.split(jax.random.fold_in(key, 3))
    noise_part = jax.random.normal(noise_key, (2, B, B), jnp.float32)
    levels = jnp.exp(jax.random.uniform(diag_key, (2, B), jnp.float32, math.log(3.0), math.log(6.0)))
    spread = (noise_part + jnp.swapaxes(noise_part, 1, 2)) * (0.85 / math.sqrt(B))
    return spread + levels[:, :, None] * jnp.eye(B, dtype=jnp.float32)[None]


def block_scale(rng, extent, cuts, least, largest):
    gain, own = 1.0, jax.random.fold_in(rng, 6)
    for axis_at, blocks in cuts:
        draws = jnp.exp(jax.random.uniform(jax.random.fold_in(own, axis_at), (blocks,), jnp.float32, least / len(cuts), largest / len(cuts)))
        gain = gain * jnp.repeat(draws, extent[axis_at] // blocks).reshape([-1 if axis == axis_at else 1 for axis in range(len(extent))])
    return gain


def noise(key, dims, scale, reach, shards=(), held_as=jnp.bfloat16):
    drawn = jax.random.normal(key, dims, jnp.float32) * scale
    if len(shards) > 0:
        drawn = block_scale(key, dims, shards, -0.22, 0.18) * drawn
    return jnp.clip(drawn, min=-reach, max=reach).astype(held_as)


def setup_inputs(seed: int = 0) -> dict:
    arg_keys = jax.random.split(jax.random.key(seed), 8)
    trailing_tiles = noise(arg_keys[0], (N_TILES * N_REP * SLOTS, B, B), 1.0, 6.0, ((0, 256),), jnp.float32)
    panel_rows = noise(arg_keys[1], (N_TILES * RPD, B, 2 * B), 0.5, 3.0, ((0, 64),), jnp.float32)
    pivot_blocks = draw_pivot_blocks(jax.random.fold_in(arg_keys[7], 71), 0)
    coupling = noise(arg_keys[3], (B, B), (4 * B) ** -0.5, 0.1875, (), jnp.float32)
    row_ids = draw_row_ids(jax.random.fold_in(arg_keys[7], 71), 0)
    membership = draw_membership(jax.random.fold_in(arg_keys[7], 71), 0)
    tile_pairs = draw_tile_pairs(jax.random.fold_in(arg_keys[7], 71), 0)
    return dict(trailing_tiles=trailing_tiles, panel_rows=panel_rows, pivot_blocks=pivot_blocks, coupling=coupling, row_ids=row_ids, membership=membership, tile_pairs=tile_pairs)


def pivot_factor(matrix):
    lower_factor = jnp.linalg.cholesky(matrix)
    pivots = jnp.diagonal(lower_factor)
    identity = jnp.eye(matrix.shape[0], dtype=matrix.dtype)
    inverse = jax.scipy.linalg.solve_triangular(lower_factor, identity, lower=True)
    return (inverse.T / pivots[None, :], pivots * pivots)

def panel_factors(panel_rows, pivot_blocks, coupling, usable):
    panel_width = pivot_blocks.shape[1]
    solve_one, diag_one = pivot_factor(pivot_blocks[0])
    coupled = jnp.dot(coupling, solve_one, precision=lax.Precision.HIGHEST)
    schur = pivot_blocks[1] - jnp.dot(coupled * diag_one[None, :], coupled.T, precision=lax.Precision.HIGHEST)
    solve_two, diag_two = pivot_factor(schur)
    first = jnp.einsum('rik,kj->rij', panel_rows[:, :, :panel_width], solve_one, precision=lax.Precision.HIGHEST)
    second_raw = panel_rows[:, :, panel_width:] - jnp.einsum('rik,jk->rij', first * diag_one[None, None, :], coupled, precision=lax.Precision.HIGHEST)
    second = jnp.einsum('rik,kj->rij', second_raw, solve_two, precision=lax.Precision.HIGHEST)
    joined = jnp.concatenate([first, second], axis=2)
    factors = jnp.where(usable[:, None, None], joined, jnp.zeros_like(joined))
    return (factors, diag_one, diag_two)

def reference(trailing_tiles, panel_rows, pivot_blocks, coupling, row_ids, membership, tile_pairs):
    factors, diag_one, diag_two = panel_factors(panel_rows, pivot_blocks, coupling, row_ids < NB)
    scales = jnp.concatenate([diag_one, diag_two])
    panel_width = pivot_blocks.shape[1]
    placed = jnp.zeros((NB + 1, panel_width, 2 * panel_width), factors.dtype).at[row_ids].set(factors)
    extended = jnp.concatenate([membership, jnp.full((N_TILES, 1), NB, membership.dtype)], axis=1)
    tiles_grouped = trailing_tiles.reshape(N_TILES, N_REP * SLOTS, panel_width, panel_width)
    pairs_grouped = tile_pairs.reshape(N_TILES, N_REP * SLOTS, 2)

    def one_group(operands):
        tile_block, pair_block, listed = operands
        left_rows = placed[listed[pair_block[:, 0]]] * scales[None, None, :]
        right_rows = placed[listed[pair_block[:, 1]]]
        return tile_block - jnp.einsum('sik,sjk->sij', left_rows, right_rows, precision=lax.Precision.HIGHEST)
    updated = lax.map(one_group, (tiles_grouped, pairs_grouped, extended))
    return (updated.reshape(trailing_tiles.shape), factors, jnp.stack([diag_one, diag_two]))
```

```python
import functools

import jax
import jax.numpy as jnp
from jax import lax
from jax.experimental import pallas as pl
from jax.experimental.pallas import tpu as pltpu
from jax.sharding import PartitionSpec as P

NB = 96
W = 64
F32 = jnp.float32
BF = jnp.bfloat16
HI = lax.Precision.HIGHEST


def dot(a, b):
    return lax.dot_general(a, b, (((1,), (0,)), ((), ())), precision=HI, preferred_element_type=F32)


def dot_nt(a, b):
    return lax.dot_general(a, b, (((1,), (1,)), ((), ())), precision=HI, preferred_element_type=F32)


def split(x):
    hi = x.astype(BF)
    return hi, (x - hi.astype(F32)).astype(BF)


def dot3(ah, al, bh, bl, nt=False):
    dims = (((1,), (1 if nt else 0,)), ((), ()))
    f = functools.partial(lax.dot_general, dimension_numbers=dims, preferred_element_type=F32)
    return f(ah, bh) + (f(ah, bl) + f(al, bh))


def eliminate(state, diag, at, n):
    lo, up = at * W, (at + 1) * W
    block = state[lo:up, lo:up]
    rows = lax.broadcasted_iota(jnp.int32, (W, 2 * W), 0)
    lanes = lax.broadcasted_iota(jnp.int32, (W, 2 * W), 1)
    eye = (lax.broadcasted_iota(jnp.int32, (W, W), 0) == lax.broadcasted_iota(jnp.int32, (W, W), 1))
    aug = jnp.concatenate([block, eye.astype(F32)], axis=1)
    for k in range(W):
        column = jnp.broadcast_to(aug[:, k : k + 1], (W, 2 * W))
        pivot_row = aug[k : k + 1, :] / column[k : k + 1, :]
        aug = aug - jnp.where(rows > k, column, 0.0) * pivot_row
    inverse = aug[:, W:]
    on_diag = jnp.where(rows == lanes, aug, 0.0)
    d_col = jnp.sum(on_diag, axis=1, keepdims=True)
    diag[0:1, (at % 2) * W : (at % 2 + 1) * W] = jnp.sum(on_diag, axis=0, keepdims=True)[:, :W]
    width = state.shape[1]
    col = lax.broadcasted_iota(jnp.int32, (W, width), 1)
    row = lax.broadcasted_iota(jnp.int32, (W, width), 0)
    own = state[lo:up, :]
    own = jnp.where((col >= lo) & (col < up), (col - lo == row).astype(F32), own)
    if up < n:
        below = dot(dot_nt(state[up:n, lo:up], inverse), inverse / d_col)
        base = state[up:n, :]
        bcol = lax.broadcasted_iota(jnp.int32, base.shape, 1)
        base = jnp.where((bcol >= lo) & (bcol < up), 0.0, base)
        state[up:n, :] = base - dot(below, own)
    state[lo:up, :] = jnp.where(col < up, dot(inverse, own), 0.0)


def first_kernel(pivot, coupling, state, diag):
    h = coupling.shape[0]
    state[:h, :h] = pivot[0]
    state[h:, :h] = coupling[...]
    state[:h, h:] = coupling[...].T
    state[h:, h:] = pivot[1]
    for at in (0, 1):
        eliminate(state, diag, at, 2 * h)


def middle_kernel(at, before, state, diag):
    state[...] = before[...]
    for p in (at, at + 1):
        eliminate(state, diag, p, state.shape[0])


def last_kernel(at, before, high, low, diag, state):
    state[...] = before[...]
    for p in (at, at + 1):
        eliminate(state, diag, p, state.shape[0])
    hi, lo = split(state[...].T)
    high[...] = hi
    low[...] = lo


def cost(flops, nbytes):
    return pl.CostEstimate(flops=int(flops), bytes_accessed=int(nbytes), transcendentals=0)


def factorize(pivot_blocks, coupling):
    n = 2 * coupling.shape[0]
    full = jax.ShapeDtypeStruct((n, n), F32)
    half = jax.ShapeDtypeStruct((n, n), BF)
    dshape = jax.ShapeDtypeStruct((1, 2 * W), F32)
    work = cost(6e9, 2 * n * n * 4)
    diags = []
    state, d = pl.pallas_call(first_kernel, out_shape=(full, dshape), cost_estimate=work, name="panels0")(pivot_blocks, coupling)
    diags.append(d)
    for at in (2, 4):
        state, d = pl.pallas_call(
            functools.partial(middle_kernel, at), out_shape=(full, dshape), cost_estimate=work, name=f"panels{at}"
        )(state)
        diags.append(d)
    high, low, d = pl.pallas_call(
        functools.partial(last_kernel, 6),
        out_shape=(half, half, dshape),
        scratch_shapes=[pltpu.VMEM((n, n), F32)],
        cost_estimate=work,
        name="panels6",
    )(state)
    diags.append(d)
    return high, low, jnp.concatenate(diags, axis=1)


def apply_inverse(x, high, low):
    h = high.shape[0] // 2
    xh, xl = split(x)
    first = dot3(xh[:, :h], xl[:, :h], high[:h, :h], low[:h, :h])
    second = dot3(xh, xl, high[:, h:], low[:, h:])
    return jnp.concatenate([first, second], axis=1)


def own_kernel(keep, x, high, low, diag, out):
    i = pl.program_id(0)
    y = apply_inverse(x[0], high, low) / diag[...]
    out[0] = jnp.where(keep[i] > 0, y, 0.0)


def own_factors(panel_rows, high, low, diag, usable):
    slots, b, n = panel_rows.shape
    const = lambda i, k: (0, 0)
    return pl.pallas_call(
        own_kernel,
        out_shape=jax.ShapeDtypeStruct(panel_rows.shape, F32),
        grid_spec=pltpu.PrefetchScalarGridSpec(
            num_scalar_prefetch=1,
            grid=(slots,),
            in_specs=[
                pl.BlockSpec((1, b, n), lambda i, k: (i, 0, 0)),
                pl.BlockSpec((n, n), const),
                pl.BlockSpec((n, n), const),
                pl.BlockSpec((1, n), const),
            ],
            out_specs=pl.BlockSpec((1, b, n), lambda i, k: (i, 0, 0)),
        ),
        cost_estimate=cost(slots * b * n * n * 6, slots * b * n * 8),
        name="own_factors",
    )(usable.astype(jnp.int32), panel_rows, high, low, diag)


def pick_kernel(slots, table, out, sems):
    count = out.shape[0]
    copies = [pltpu.make_async_copy(table.at[slots[g]], out.at[g], sems.at[g]) for g in range(count)]
    for c in copies:
        c.start()
    for c in copies:
        c.wait()


def pick(table, slots):
    count = slots.shape[0]
    shape = (count,) + table.shape[1:]
    return pl.pallas_call(
        pick_kernel,
        out_shape=jax.ShapeDtypeStruct(shape, F32),
        grid_spec=pltpu.PrefetchScalarGridSpec(
            num_scalar_prefetch=1,
            grid=(),
            in_specs=[pl.BlockSpec(memory_space=pl.ANY)],
            out_specs=pl.BlockSpec(memory_space=pltpu.VMEM),
            scratch_shapes=[pltpu.SemaphoreType.DMA((count,))],
        ),
        cost_estimate=cost(0, 2 * 4 * count * shape[1] * shape[2]),
        name="pick",
    )(slots, table)


def solve_kernel(group, half, info, x, high, low, diag, *refs):
    oh, ol = refs[-2:]
    i = pl.program_id(0)
    rows = x.shape[1]
    y = apply_inverse(x[...].reshape(group * rows, x.shape[2]), high, low)
    y = jnp.where(i * group < half, y, y / diag[...])
    y = y.reshape(group, rows, x.shape[2])
    for g in range(group):
        part = jnp.where(info[1 + i * group + g] > 0, y[g], 0.0)
        hi, lo = split(part)
        oh[g] = hi
        ol[g] = lo


def solve_rows(x, high, low, diag, quarter, valid, b, previous):
    count, rows, n = x.shape
    group = 4
    info = jnp.concatenate([quarter[None], valid]).astype(jnp.int32)
    const = lambda i, s: (0, 0)
    place = pl.BlockSpec((group, rows, n), lambda i, s: (i, s[0], 0))
    shape = jax.ShapeDtypeStruct((count, b, n), BF)
    extra = () if previous is None else tuple(previous)
    return pl.pallas_call(
        functools.partial(solve_kernel, group, count // 2),
        out_shape=(shape, shape),
        grid_spec=pltpu.PrefetchScalarGridSpec(
            num_scalar_prefetch=1,
            grid=(count // group,),
            in_specs=[
                pl.BlockSpec((group, rows, n), lambda i, s: (i, 0, 0)),
                pl.BlockSpec((n, n), const),
                pl.BlockSpec((n, n), const),
                pl.BlockSpec((1, n), const),
            ]
            + [pl.BlockSpec(memory_space=pl.ANY)] * len(extra),
            out_specs=(place, place),
        ),
        input_output_aliases={5: 0, 6: 1} if extra else {},
        cost_estimate=cost(count * rows * n * n * 4.5, count * rows * n * 8),
        name="solve_rows",
    )(info, x, high, low, diag, *extra)


def update_kernel(info, tile, lh, ll, rh, rl, out):
    k = pl.program_id(0)
    live = info[2, k] > 0

    @pl.when(live)
    def _():
        out[0] = tile[0] - dot3(lh[0], ll[0], rh[0], rl[0], nt=True)

    @pl.when(jnp.logical_not(live))
    def _():
        out[0] = tile[0]


def update_tiles(tiles, high, low, pairs):
    slots, b, _ = tiles.shape
    count, _, n = high.shape
    left = jnp.minimum(pairs[:, 0], count - 1)
    right = jnp.minimum(pairs[:, 1], count - 1)
    info = jnp.stack([left, right, (pairs[:, 0] < count).astype(jnp.int32)])
    lspec = pl.BlockSpec((1, b, n), lambda k, s: (s[0, k], 0, 0))
    rspec = pl.BlockSpec((1, b, n), lambda k, s: (s[1, k], 0, 0))
    tspec = pl.BlockSpec((1, b, b), lambda k, s: (k, 0, 0))
    return pl.pallas_call(
        update_kernel,
        out_shape=jax.ShapeDtypeStruct(tiles.shape, F32),
        grid_spec=pltpu.PrefetchScalarGridSpec(
            num_scalar_prefetch=1,
            grid=(slots,),
            in_specs=[tspec, lspec, lspec, rspec, rspec],
            out_specs=tspec,
        ),
        cost_estimate=cost(slots * b * b * n * 6, slots * b * (8 * b + 8 * n)),
        name="update_tiles",
    )(info, tiles, high, low, high, low)


def turn_perm(tiles, reps, step):
    return [
        (t * reps + x, t * reps + (x + (step if t % 2 == 0 else -step)) % reps) for t in range(tiles) for x in range(reps)
    ]


def per_device(tiles, reps, trailing_tiles, panel_rows, pivot_blocks, coupling, row_ids, membership, tile_pairs):
    owned_slots, b, n = panel_rows.shape
    tile_index = lax.axis_index("tiles")
    rep_index = lax.axis_index("rep")
    own_ids = lax.dynamic_slice_in_dim(row_ids, tile_index * owned_slots, owned_slots)
    wanted = lax.dynamic_index_in_dim(membership, tile_index, 0, keepdims=False)
    match = wanted[:, None] == row_ids[None, :]
    position = jnp.arange(row_ids.shape[0], dtype=jnp.int32)
    slots = jnp.max(jnp.where(match, position[None, :], 0), axis=1)
    valid = (wanted < NB).astype(jnp.int32)

    quarter = b // reps
    my_rows = lax.dynamic_slice_in_dim(panel_rows, rep_index * quarter, quarter, 1)
    gathered = lax.all_gather(my_rows, "tiles", axis=0, tiled=True)
    high, low, diag = factorize(pivot_blocks, coupling)
    factors = own_factors(panel_rows, high, low, diag, own_ids < NB)

    mine = pick(gathered, slots)
    both = ("tiles", "rep")
    ahead, back = turn_perm(tiles, reps, 1), turn_perm(tiles, reps, -1)
    one = lax.ppermute(mine, both, ahead)
    other = lax.ppermute(mine, both, back)
    far = lax.ppermute(one, both, ahead)
    turn = 1 - 2 * (tile_index % 2)
    solved = None
    for x, shift in ((mine, 0), (one, -turn), (other, turn), (far, 2)):
        at = (rep_index + shift + reps) % reps
        solved = solve_rows(x, high, low, diag, at, valid, b, solved)
    updated = update_tiles(trailing_tiles, *solved, tile_pairs)
    return (updated, factors, diag.reshape(2, b))


def solution(mesh):
    return jax.shard_map(
        functools.partial(per_device, mesh.shape["tiles"], mesh.shape["rep"]),
        mesh=mesh,
        in_specs=(
            P(("tiles", "rep"), None, None),
            P("tiles", None, None),
            P(),
            P(),
            P(),
            P(),
            P(("tiles", "rep"), None),
        ),
        out_specs=(P(("tiles", "rep"), None, None), P("tiles", None, None), P()),
        check_vma=False,
    )
```

```python
import functools

import jax
import jax.numpy as jnp
from jax import lax
from jax.experimental import pallas as pl
from jax.experimental.pallas import tpu as pltpu
from jax.sharding import PartitionSpec as P

NB = 96
NY, NZ = 4, 8
SPLIT = 128
W = 64
GROUP = 4
F32 = jnp.float32
BF = jnp.bfloat16
HI = lax.Precision.HIGHEST


def dot(a, b):
    return lax.dot_general(a, b, (((1,), (0,)), ((), ())), precision=HI, preferred_element_type=F32)


def dot_nt(a, b):
    return lax.dot_general(a, b, (((1,), (1,)), ((), ())), precision=HI, preferred_element_type=F32)


def split(x):
    hi = x.astype(BF)
    return hi, (x - hi.astype(F32)).astype(BF)


def dot3(ah, al, bh, bl, nt=False):
    dims = (((1,), (1 if nt else 0,)), ((), ()))
    f = functools.partial(lax.dot_general, dimension_numbers=dims, preferred_element_type=F32)
    return f(ah, bh) + (f(ah, bl) + f(al, bh))


def eliminate(state, diag, at, n):
    lo, up = at * W, (at + 1) * W
    block = state[lo:up, lo:up]
    rows = lax.broadcasted_iota(jnp.int32, (W, 2 * W), 0)
    lanes = lax.broadcasted_iota(jnp.int32, (W, 2 * W), 1)
    eye = (lax.broadcasted_iota(jnp.int32, (W, W), 0) == lax.broadcasted_iota(jnp.int32, (W, W), 1))
    aug = jnp.concatenate([block, eye.astype(F32)], axis=1)
    for first in range(0, W, GROUP):
        columns = [jnp.broadcast_to(aug[:, k : k + 1], (W, 2 * W)) for k in range(first, first + GROUP)]
        for k in range(first, first + GROUP):
            column = columns[k - first]
            reciprocal = 1.0 / column[k : k + 1, :]
            below = jnp.where(rows > k, column, 0.0)
            aug = aug - below * (aug[k : k + 1, :] * reciprocal)
            for later in range(k + 1 - first, GROUP):
                columns[later] = columns[later] - below * (columns[later][k : k + 1, :] * reciprocal)
    inverse = aug[:, W:]
    on_diag = jnp.where(rows == lanes, aug, 0.0)
    d_col = jnp.sum(on_diag, axis=1, keepdims=True)
    diag[0:1, (at % 2) * W : (at % 2 + 1) * W] = jnp.sum(on_diag, axis=0, keepdims=True)[:, :W]
    width = state.shape[1]
    col = lax.broadcasted_iota(jnp.int32, (W, width), 1)
    row = lax.broadcasted_iota(jnp.int32, (W, width), 0)
    own = state[lo:up, :]
    own = jnp.where((col >= lo) & (col < up), (col - lo == row).astype(F32), own)
    if up < n:
        below = dot(dot_nt(state[up:n, lo:up], inverse), inverse / d_col)
        base = state[up:n, :]
        bcol = lax.broadcasted_iota(jnp.int32, base.shape, 1)
        base = jnp.where((bcol >= lo) & (bcol < up), 0.0, base)
        state[up:n, :] = base - dot(below, own)
    state[lo:up, :] = jnp.where(col < up, dot(inverse, own), 0.0)


def first_kernel(pivot, coupling, state, diag):
    h = coupling.shape[0]
    state[:h, :h] = pivot[0]
    state[h:, :h] = coupling[...]
    state[:h, h:] = coupling[...].T
    state[h:, h:] = pivot[1]
    for at in (0, 1):
        eliminate(state, diag, at, 2 * h)


def middle_kernel(at, before, state, diag):
    state[...] = before[...]
    for p in (at, at + 1):
        eliminate(state, diag, p, state.shape[0])


def last_kernel(at, before, d0, d1, d2, high, low, full_high, full_low, diag, state, last):
    state[...] = before[...]
    for p in (at, at + 1):
        eliminate(state, last, p, state.shape[0])
    for p, d in enumerate((d0, d1, d2, last)):
        diag[0:1, p * 2 * W : (p + 1) * 2 * W] = d[...]
    inverse = state[...]
    turned = inverse.T
    high[...], low[...] = split(turned)
    full_high[...], full_low[...] = split(dot(turned / diag[...], inverse))


def cost(flops, nbytes):
    return pl.CostEstimate(flops=int(flops), bytes_accessed=int(nbytes), transcendentals=0)


def factorize(pivot_blocks, coupling):
    n = 2 * coupling.shape[0]
    full = jax.ShapeDtypeStruct((n, n), F32)
    half = jax.ShapeDtypeStruct((n, n), BF)
    dshape = jax.ShapeDtypeStruct((1, 2 * W), F32)
    work = cost(6e9, 2 * n * n * 4)
    diags = []
    state, d = pl.pallas_call(first_kernel, out_shape=(full, dshape), cost_estimate=work, name="panels0")(pivot_blocks, coupling)
    diags.append(d)
    for at in (2, 4):
        state, d = pl.pallas_call(
            functools.partial(middle_kernel, at), out_shape=(full, dshape), cost_estimate=work, name=f"panels{at}"
        )(state)
        diags.append(d)
    return pl.pallas_call(
        functools.partial(last_kernel, 6),
        out_shape=(half, half, half, half, jax.ShapeDtypeStruct((1, n), F32)),
        scratch_shapes=[pltpu.VMEM((n, n), F32), pltpu.VMEM((1, 2 * W), F32)],
        cost_estimate=work,
        name="panels6",
    )(state, *diags)


def apply_inverse(x, high, low):
    h = high.shape[0] // 2
    xh, xl = split(x)
    first = dot3(xh[:, :h], xl[:, :h], high[:h, :h], low[:h, :h])
    second = dot3(xh, xl, high[:, h:], low[:, h:])
    return jnp.concatenate([first, second], axis=1)


def own_kernel(keep, x, high, low, diag, out):
    i = pl.program_id(0)
    y = apply_inverse(x[0], high, low) / diag[...]
    out[0] = jnp.where(keep[i] > 0, y, 0.0)


def own_factors(panel_rows, high, low, diag, usable):
    slots, b, n = panel_rows.shape
    const = lambda i, k: (0, 0)
    return pl.pallas_call(
        own_kernel,
        out_shape=jax.ShapeDtypeStruct(panel_rows.shape, F32),
        grid_spec=pltpu.PrefetchScalarGridSpec(
            num_scalar_prefetch=1,
            grid=(slots,),
            in_specs=[
                pl.BlockSpec((1, b, n), lambda i, k: (i, 0, 0)),
                pl.BlockSpec((n, n), const),
                pl.BlockSpec((n, n), const),
                pl.BlockSpec((1, n), const),
            ],
            out_specs=pl.BlockSpec((1, b, n), lambda i, k: (i, 0, 0)),
        ),
        cost_estimate=cost(slots * b * n * n * 6, slots * b * n * 8),
        name="own_factors",
    )(usable.astype(jnp.int32), panel_rows, high, low, diag)


def pick_kernel(place, *refs):
    nz, ny = 8, 4
    zy = refs[:nz]
    yz = refs[nz : nz + ny]
    outs = refs[nz + ny : nz + ny + 2]
    sems = refs[nz + ny + 2]
    count, rows, _ = outs[0].shape
    half = rows // 2

    def copy(color, which, g, source, at):
        target = outs[which].at[g, pl.ds(color * half, half)]
        return pltpu.make_async_copy(source.at[at], target, sems.at[color, which, g])

    for which in range(2):

        @pl.loop(0, count)
        def _(g):
            ez, ey, slot = place[which, 0, g], place[which, 1, g], place[which, 2, g]
            for e in range(nz):

                @pl.when(ez == e)
                def _():
                    copy(0, which, g, zy[e], ey * 2 + slot).start()

            for e in range(ny):

                @pl.when(ey == e)
                def _():
                    copy(1, which, g, yz[e], ez * 2 + slot).start()

    for which in range(2):

        @pl.loop(0, count)
        def _(g):
            copy(0, which, g, zy[0], 0).wait()
            copy(1, which, g, yz[0], 0).wait()


def pick(zy, yz, place, rows, n):
    count = place.shape[2]
    shape = jax.ShapeDtypeStruct((count, rows, n), F32)
    return pl.pallas_call(
        pick_kernel,
        out_shape=(shape, shape),
        grid_spec=pltpu.PrefetchScalarGridSpec(
            num_scalar_prefetch=1,
            grid=(),
            in_specs=[pl.BlockSpec(memory_space=pl.ANY)] * (len(zy) + len(yz)),
            out_specs=(pl.BlockSpec(memory_space=pltpu.VMEM),) * 2,
            scratch_shapes=[pltpu.SemaphoreType.DMA((2, 2, count))],
        ),
        cost_estimate=cost(0, 4 * 4 * count * rows * n),
        name="pick",
    )(place, *zy, *yz)


def update_kernel(info, tile, full_high, full_low, p0, p1, p2, p3, table, out, stage, lh, ll, rh, rl, sems):
    k = pl.program_id(0)
    count, b, n = stage.shape
    half = count // 2
    rows = p0.shape[1]
    tail = table.shape[1]

    @pl.when(k == 0)
    def _():
        parts = [
            pltpu.make_async_copy(p, stage.at[:, pl.ds(pl.multiple_of(info[3, i] * rows, rows), rows), :], sems.at[count + i])
            for i, p in enumerate((p0, p1, p2, p3))
        ]
        for c in parts:
            c.start()

        def rest(g):
            return pltpu.make_async_copy(table.at[info[4, g]], stage.at[g, pl.ds(b - tail, tail), :], sems.at[g])

        @pl.loop(0, count)
        def _(g):
            rest(g).start()

        for c in parts:
            c.wait()

        @pl.loop(0, half)
        def _(g):
            rest(g).wait()
            x = jnp.where(info[5, g] > 0, stage[g], 0.0)
            xh, xl = split(x)
            yh, yl = split(dot3(xh, xl, full_high[...], full_low[...]))
            lh[g] = yh
            ll[g] = yl

        @pl.loop(half, count)
        def _(g):
            rest(g).wait()
            x = jnp.where(info[5, g] > 0, stage[g], 0.0)
            xh, xl = split(x)
            rh[g - half] = xh
            rl[g - half] = xl

    live = info[2, k] > 0

    @pl.when(live)
    def _():
        i, j = info[0, k], info[1, k]
        out[0] = tile[0] - dot3(lh[i], ll[i], rh[j], rl[j], nt=True)

    @pl.when(jnp.logical_not(live))
    def _():
        out[0] = tile[0]


def update_tiles(tiles, full_high, full_low, parts, quarters, table, slots, valid, pairs):
    total, b, _ = tiles.shape
    count = slots.shape[0]
    half = count // 2
    n = full_high.shape[0]
    widest = max(total, count)
    fit = lambda v: jnp.pad(v.astype(jnp.int32), (0, widest - v.shape[0]))
    info = jnp.stack(
        [
            fit(jnp.minimum(pairs[:, 0], half - 1)),
            fit(jnp.clip(pairs[:, 1] - half, 0, half - 1)),
            fit(pairs[:, 0] < count),
            fit(jnp.stack(quarters)),
            fit(slots),
            fit(valid),
        ]
    )
    tspec = pl.BlockSpec((1, b, b), lambda k, s: (k, 0, 0))
    whole = pl.BlockSpec((n, n), lambda k, s: (0, 0))
    anywhere = pl.BlockSpec(memory_space=pl.ANY)
    operand = pltpu.VMEM((half, b, n), BF)
    return pl.pallas_call(
        update_kernel,
        out_shape=jax.ShapeDtypeStruct(tiles.shape, F32),
        grid_spec=pltpu.PrefetchScalarGridSpec(
            num_scalar_prefetch=1,
            grid=(total,),
            in_specs=[tspec, whole, whole] + [anywhere] * 5,
            out_specs=tspec,
            scratch_shapes=[pltpu.VMEM((count, b, n), F32)]
            + [operand] * 4
            + [pltpu.SemaphoreType.DMA((count + 4,))],
        ),
        compiler_params=pltpu.CompilerParams(vmem_limit_bytes=40 * 2**20),
        cost_estimate=cost(total * b * b * n * 6 + half * b * n * n * 6, total * b * 8 * b + count * b * n * 4),
        name="update_tiles",
    )(info, tiles, full_high, full_low, *parts, table)


def turned(core, step):
    return step if core == 0 else -step


def tile_of(y, z, core):
    return ((y % NY) * NZ + z % NZ) * 2 + core


def chips():
    return [(y, z, c) for y in range(NY) for z in range(NZ) for c in range(2)]


def z_perm(step):
    return [(tile_of(y, z, c), tile_of(y, z + turned(c, step), c)) for y, z, c in chips()]


def y_perm(step):
    return [(tile_of(y, z, c), tile_of(y + turned(c, step), z, c)) for y, z, c in chips()]


def x_perm(tiles, reps, step):
    return [(t * reps + x, t * reps + (x + turned(t % 2, step)) % reps) for t in range(tiles) for x in range(reps)]


def ring(block, size, ahead, back):
    near, far = [block], [block]
    for k in range(size // 2):
        near.append(lax.ppermute(near[-1], "tiles", ahead))
        if k < size // 2 - 1:
            far.append(lax.ppermute(far[-1], "tiles", back))
    return near + far[:0:-1]


def per_device(tiles, reps, trailing_tiles, panel_rows, pivot_blocks, coupling, row_ids, membership, tile_pairs):
    owned_slots, b, n = panel_rows.shape
    tile_index = lax.axis_index("tiles")
    rep_index = lax.axis_index("rep")
    core, my_z, my_y = tile_index % 2, (tile_index // 2) % NZ, tile_index // (2 * NZ)
    turn = 1 - 2 * core
    own_ids = lax.dynamic_slice_in_dim(row_ids, tile_index * owned_slots, owned_slots)

    quarter = SPLIT // reps
    half = quarter // 2
    gathered = lax.all_gather(panel_rows[:, SPLIT:], "tiles", axis=0, tiled=True)
    top = lax.dynamic_slice_in_dim(panel_rows, rep_index * quarter, half, 1)
    low_rows = lax.dynamic_slice_in_dim(panel_rows, rep_index * quarter + half, half, 1)
    za, zb, ya, yb = z_perm(1), z_perm(-1), y_perm(1), y_perm(-1)
    zy = ring(jnp.concatenate(ring(top, NY, ya, yb), axis=0), NZ, za, zb)
    yz = ring(jnp.concatenate(ring(low_rows, NZ, za, zb), axis=0), NY, ya, yb)

    both_lists = lax.dynamic_slice_in_dim(membership, (tile_index // 2) * 2, 2, 0)
    match = both_lists[:, :, None] == row_ids[None, None, :]
    position = jnp.arange(row_ids.shape[0], dtype=jnp.int32)
    where = jnp.max(jnp.where(match, position[None, None, :], 0), axis=2)
    where = jnp.where(core == 0, where, where[::-1])
    slots = where[0]
    valid = lax.dynamic_index_in_dim(membership, tile_index, 0, keepdims=False) < NB
    ez = (turn * (my_z - (where // 4) % NZ)) % NZ
    ey = (turn * (my_y - where // (4 * NZ))) % NY
    place = jnp.stack([ez, ey, where % 2], axis=1)
    here = (slots // 2) % 2 == core

    mine, theirs = pick(zy, yz, place, quarter, n)
    swap = [(t, t ^ 1) for t in range(tiles)]
    mine = jnp.where(here[:, None, None], mine, lax.ppermute(theirs, "tiles", swap))
    both = ("tiles", "rep")
    ahead, back = x_perm(tiles, reps, 1), x_perm(tiles, reps, -1)
    one = lax.ppermute(mine, both, ahead)
    other = lax.ppermute(mine, both, back)
    far = lax.ppermute(one, both, ahead)
    quarters = [(rep_index + shift + reps) % reps for shift in (0, -turn, turn, 2)]

    high, low, full_high, full_low, diag = factorize(pivot_blocks, coupling)
    factors = own_factors(panel_rows, high, low, diag, own_ids < NB)
    updated = update_tiles(
        trailing_tiles, full_high, full_low, (mine, one, other, far), quarters, gathered, slots, valid, tile_pairs
    )
    return (updated, factors, diag.reshape(2, b))


def solution(mesh):
    return jax.shard_map(
        functools.partial(per_device, mesh.shape["tiles"], mesh.shape["rep"]),
        mesh=mesh,
        in_specs=(
            P(("tiles", "rep"), None, None),
            P("tiles", None, None),
            P(),
            P(),
            P(),
            P(),
            P(("tiles", "rep"), None),
        ),
        out_specs=(P(("tiles", "rep"), None, None), P("tiles", None, None), P()),
        check_vma=False,
    )
```

```python
import functools

import jax
import jax.numpy as jnp
from jax import lax
from jax.experimental import pallas as pl
from jax.experimental.pallas import tpu as pltpu
from jax.sharding import PartitionSpec as P


NB = 96
NY, NZ = 4, 8
SPLIT = 128
W = 64
GROUP = 4
F32 = jnp.float32
BF = jnp.bfloat16
HI = lax.Precision.HIGHEST


def dot(a, b):
    return lax.dot_general(a, b, (((1,), (0,)), ((), ())), precision=HI, preferred_element_type=F32)


def dot_nt(a, b):
    return lax.dot_general(a, b, (((1,), (1,)), ((), ())), precision=HI, preferred_element_type=F32)


def split(x):
    hi = x.astype(BF)
    return hi, (x - hi.astype(F32)).astype(BF)


def dot3(ah, al, bh, bl, nt=False):
    dims = (((1,), (1 if nt else 0,)), ((), ()))
    f = functools.partial(lax.dot_general, dimension_numbers=dims, preferred_element_type=F32)
    return f(ah, bh) + (f(ah, bl) + f(al, bh))


def eliminate(state, diag, at, n):
    lo, up = at * W, (at + 1) * W
    block = state[lo:up, lo:up]
    rows = lax.broadcasted_iota(jnp.int32, (W, 2 * W), 0)
    lanes = lax.broadcasted_iota(jnp.int32, (W, 2 * W), 1)
    eye = (lax.broadcasted_iota(jnp.int32, (W, W), 0) == lax.broadcasted_iota(jnp.int32, (W, W), 1))
    aug = jnp.concatenate([block, eye.astype(F32)], axis=1)
    for first in range(0, W, GROUP):
        columns = [jnp.broadcast_to(aug[:, k : k + 1], (W, 2 * W)) for k in range(first, first + GROUP)]
        for k in range(first, first + GROUP):
            column = columns[k - first]
            reciprocal = 1.0 / column[k : k + 1, :]
            below = jnp.where(rows > k, column, 0.0)
            aug = aug - below * (aug[k : k + 1, :] * reciprocal)
            for later in range(k + 1 - first, GROUP):
                columns[later] = columns[later] - below * (columns[later][k : k + 1, :] * reciprocal)
    inverse = aug[:, W:]
    on_diag = jnp.where(rows == lanes, aug, 0.0)
    d_col = jnp.sum(on_diag, axis=1, keepdims=True)
    diag[0:1, (at % 2) * W : (at % 2 + 1) * W] = jnp.sum(on_diag, axis=0, keepdims=True)[:, :W]
    width = state.shape[1]
    col = lax.broadcasted_iota(jnp.int32, (W, width), 1)
    row = lax.broadcasted_iota(jnp.int32, (W, width), 0)
    own = state[lo:up, :]
    own = jnp.where((col >= lo) & (col < up), (col - lo == row).astype(F32), own)
    if up < n:
        below = dot(dot_nt(state[up:n, lo:up], inverse), inverse / d_col)
        base = state[up:n, :]
        bcol = lax.broadcasted_iota(jnp.int32, base.shape, 1)
        base = jnp.where((bcol >= lo) & (bcol < up), 0.0, base)
        state[up:n, :] = base - dot(below, own)
    state[lo:up, :] = jnp.where(col < up, dot(inverse, own), 0.0)


def first_kernel(pivot, coupling, state, diag):
    h = coupling.shape[0]
    state[:h, :h] = pivot[0]
    state[h:, :h] = coupling[...]
    state[:h, h:] = coupling[...].T
    state[h:, h:] = pivot[1]
    for at in (0, 1):
        eliminate(state, diag, at, 2 * h)


def middle_kernel(at, before, state, diag):
    state[...] = before[...]
    for p in (at, at + 1):
        eliminate(state, diag, p, state.shape[0])


def last_kernel(at, before, d0, d1, d2, high, low, full_high, full_low, diag, state, last):
    state[...] = before[...]
    for p in (at, at + 1):
        eliminate(state, last, p, state.shape[0])
    for p, d in enumerate((d0, d1, d2, last)):
        diag[0:1, p * 2 * W : (p + 1) * 2 * W] = d[...]
    inverse = state[...]
    turned = inverse.T
    high[...], low[...] = split(turned)
    full_high[...], full_low[...] = split(dot(turned / diag[...], inverse))


def cost(flops, nbytes):
    return pl.CostEstimate(flops=int(flops), bytes_accessed=int(nbytes), transcendentals=0)


def factorize(pivot_blocks, coupling):
    n = 2 * coupling.shape[0]
    full = jax.ShapeDtypeStruct((n, n), F32)
    half = jax.ShapeDtypeStruct((n, n), BF)
    dshape = jax.ShapeDtypeStruct((1, 2 * W), F32)
    work = cost(6e9, 2 * n * n * 4)
    diags = []
    state, d = pl.pallas_call(first_kernel, out_shape=(full, dshape), cost_estimate=work, name="panels0")(pivot_blocks, coupling)
    diags.append(d)
    for at in (2, 4):
        state, d = pl.pallas_call(
            functools.partial(middle_kernel, at), out_shape=(full, dshape), cost_estimate=work
        )(state)
        diags.append(d)
    return pl.pallas_call(
        functools.partial(last_kernel, 6),
        out_shape=(half, half, half, half, jax.ShapeDtypeStruct((1, n), F32)),
        scratch_shapes=[pltpu.VMEM((n, n), F32), pltpu.VMEM((1, 2 * W), F32)],
        cost_estimate=work,
        name="panels6",
    )(state, *diags)


def apply_inverse(x, high, low):
    h = high.shape[0] // 2
    xh, xl = split(x)
    first = dot3(xh[:, :h], xl[:, :h], high[:h, :h], low[:h, :h])
    second = dot3(xh, xl, high[:, h:], low[:, h:])
    return jnp.concatenate([first, second], axis=1)


def own_kernel(keep, x, high, low, diag, out):
    i = pl.program_id(0)
    y = apply_inverse(x[0], high, low) / diag[...]
    out[0] = jnp.where(keep[i] > 0, y, 0.0)


def own_factors(panel_rows, high, low, diag, usable):
    slots, b, n = panel_rows.shape
    const = lambda i, k: (0, 0)
    return pl.pallas_call(
        own_kernel,
        out_shape=jax.ShapeDtypeStruct(panel_rows.shape, F32),
        grid_spec=pltpu.PrefetchScalarGridSpec(
            num_scalar_prefetch=1,
            grid=(slots,),
            in_specs=[
                pl.BlockSpec((1, b, n), lambda i, k: (i, 0, 0)),
                pl.BlockSpec((n, n), const),
                pl.BlockSpec((n, n), const),
                pl.BlockSpec((1, n), const),
            ],
            out_specs=pl.BlockSpec((1, b, n), lambda i, k: (i, 0, 0)),
        ),
        cost_estimate=cost(slots * b * n * n * 6, slots * b * n * 8),
        name="own_factors",
    )(usable.astype(jnp.int32), panel_rows, high, low, diag)


def pick_kernel(place, *refs):
    buffers = refs[:-3]
    outs = refs[-3:-1]
    sems = refs[-1]
    count = outs[0].shape[0]

    def copy(which, g, source, at):
        return pltpu.make_async_copy(source.at[at], outs[which].at[g], sems.at[which, g])

    for which in range(2):

        @pl.loop(0, count)
        def _(g):
            for e, buffer in enumerate(buffers):

                @pl.when(place[which, 0, g] == e)
                def _():
                    copy(which, g, buffer, place[which, 1, g]).start()

    for which in range(2):

        @pl.loop(0, count)
        def _(g):
            copy(which, g, buffers[0], 0).wait()


def pick(buffers, place):
    count = place.shape[2]
    _, rows, n = buffers[0].shape
    shape = jax.ShapeDtypeStruct((count, rows, n), F32)
    return pl.pallas_call(
        pick_kernel,
        out_shape=(shape, shape),
        grid_spec=pltpu.PrefetchScalarGridSpec(
            num_scalar_prefetch=1,
            grid=(),
            in_specs=[pl.BlockSpec(memory_space=pl.ANY)] * len(buffers),
            out_specs=(pl.BlockSpec(memory_space=pltpu.VMEM),) * 2,
            scratch_shapes=[pltpu.SemaphoreType.DMA((2, count))],
        ),
        cost_estimate=cost(0, 4 * 4 * count * rows * n),
        name="pick",
    )(place, *buffers)


def prepare_kernel(valid, x, full_high, full_low, high, low):
    count, rows, n = x.shape
    half = count // 2
    step = 6

    @pl.loop(0, half // step)
    def _(i):
        at = i * step
        part = jnp.stack([jnp.where(valid[at + g] > 0, x[at + g], 0.0) for g in range(step)])
        xh, xl = split(part.reshape(step * rows, n))
        yh, yl = split(dot3(xh, xl, full_high[...], full_low[...]))
        high[pl.ds(at, step)] = yh.reshape(step, rows, n)
        low[pl.ds(at, step)] = yl.reshape(step, rows, n)

    @pl.loop(half, count)
    def _(g):
        xh, xl = split(jnp.where(valid[g] > 0, x[g], 0.0))
        high[g] = xh
        low[g] = xl


def prepare(x, full_high, full_low, valid):
    count, rows, n = x.shape
    shape = jax.ShapeDtypeStruct(x.shape, BF)
    vmem = pl.BlockSpec(memory_space=pltpu.VMEM)
    return pl.pallas_call(
        prepare_kernel,
        out_shape=(shape, shape),
        grid_spec=pltpu.PrefetchScalarGridSpec(
            num_scalar_prefetch=1, grid=(), in_specs=[vmem] * 3, out_specs=(vmem, vmem)
        ),
        cost_estimate=cost(count // 2 * rows * n * n * 6, count * rows * n * 8),
        name="prepare",
    )(valid, x, full_high, full_low)


def update_kernel(info, tile, full_high, full_low, *refs):
    parts, (table, out, stage, lh, ll, rh, rl, sems) = refs[:8], refs[8:]
    k = pl.program_id(0)
    count, tail, _ = stage.shape
    half, b, _ = lh.shape
    rows = parts[0].shape[1]
    head = b - tail
    step = 2

    @pl.when(k == 0)
    def _():
        def rest(g):
            return pltpu.make_async_copy(table.at[info[4, g]], stage.at[g], sems.at[g])

        @pl.loop(0, count)
        def _(g):
            rest(g).start()

        placed = []
        for i in range(8):
            at = pl.ds(pl.multiple_of(info[3, i // 2] * rows, rows), rows)
            left, right = ((lh, rh), (ll, rl))[i % 2]
            for side, target in enumerate((left, right)):
                source = parts[i].at[pl.ds(side * half, half)]
                placed.append(pltpu.make_async_copy(source, target.at[:, at, :], sems.at[count + 2 * i + side]))
        for c in placed:
            c.start()

        @pl.loop(0, half // step)
        def _(i):
            both = []
            for g in range(step):
                rest(i * step + g).wait()
                both.append(jnp.where(info[5, i * step + g] > 0, stage[i * step + g], 0.0))
            xh, xl = split(jnp.concatenate(both, axis=0))
            yh, yl = split(dot3(xh, xl, full_high[...], full_low[...]))
            for g in range(step):
                lh[i * step + g, head:] = yh[g * tail : (g + 1) * tail]
                ll[i * step + g, head:] = yl[g * tail : (g + 1) * tail]

        @pl.loop(half, count)
        def _(g):
            rest(g).wait()
            xh, xl = split(jnp.where(info[5, g] > 0, stage[g], 0.0))
            rh[g - half, head:] = xh
            rl[g - half, head:] = xl

        for c in placed:
            c.wait()

    live = info[2, k] > 0

    @pl.when(live)
    def _():
        i, j = info[0, k], info[1, k]
        out[0] = tile[0] - dot3(lh[i], ll[i], rh[j], rl[j], nt=True)

    @pl.when(jnp.logical_not(live))
    def _():
        out[0] = tile[0]


def update_tiles(tiles, full_high, full_low, parts, quarters, table, slots, valid, pairs):
    total, b, _ = tiles.shape
    count = slots.shape[0]
    half = count // 2
    n = full_high.shape[0]
    tail = table.shape[1]
    widest = max(total, count)
    fit = lambda v: jnp.pad(v.astype(jnp.int32), (0, widest - v.shape[0]))
    info = jnp.stack(
        [
            fit(jnp.minimum(pairs[:, 0], half - 1)),
            fit(jnp.clip(pairs[:, 1] - half, 0, half - 1)),
            fit(pairs[:, 0] < count),
            fit(jnp.stack(quarters)),
            fit(slots),
            fit(valid),
        ]
    )
    tspec = pl.BlockSpec((1, b, b), lambda k, s: (k, 0, 0))
    whole = pl.BlockSpec((n, n), lambda k, s: (0, 0))
    operand = pltpu.VMEM((half, b, n), BF)
    return pl.pallas_call(
        update_kernel,
        out_shape=jax.ShapeDtypeStruct(tiles.shape, F32),
        grid_spec=pltpu.PrefetchScalarGridSpec(
            num_scalar_prefetch=1,
            grid=(total,),
            in_specs=[tspec, whole, whole] + [pl.BlockSpec(memory_space=pl.ANY)] * (len(parts) + 1),
            out_specs=tspec,
            scratch_shapes=[pltpu.VMEM((count, tail, n), F32)]
            + [operand] * 4
            + [pltpu.SemaphoreType.DMA((count + 2 * len(parts),))],
        ),
        compiler_params=pltpu.CompilerParams(vmem_limit_bytes=58 * 2**20),
        cost_estimate=cost(total * b * b * n * 6 + half * tail * n * n * 6, total * b * 8 * b + count * tail * n * 4),
        name="update_tiles",
    )(info, tiles, full_high, full_low, *parts, table)


def turned(core, step):
    return step if core == 0 else -step


def tile_of(y, z, core):
    return ((y % NY) * NZ + z % NZ) * 2 + core


def chips():
    return [(y, z, c) for y in range(NY) for z in range(NZ) for c in range(2)]


def z_perm(step):
    return [(tile_of(y, z, c), tile_of(y, z + turned(c, step), c)) for y, z, c in chips()]


def y_perm(step):
    return [(tile_of(y, z, c), tile_of(y + turned(c, step), z, c)) for y, z, c in chips()]


def x_perm(tiles, reps, step):
    return [(t * reps + x, t * reps + (x + turned(t % 2, step)) % reps) for t in range(tiles) for x in range(reps)]


def ring(block, size, ahead, back):
    near, far = [block], [block]
    for k in range(size // 2):
        near.append(lax.ppermute(near[-1], "tiles", ahead))
        if k < size // 2 - 1:
            far.append(lax.ppermute(far[-1], "tiles", back))
    return near + far[:0:-1]


def per_device(tiles, reps, trailing_tiles, panel_rows, pivot_blocks, coupling, row_ids, membership, tile_pairs):
    owned_slots, b, _ = panel_rows.shape
    tile_index = lax.axis_index("tiles")
    rep_index = lax.axis_index("rep")
    core, my_z, my_y = tile_index % 2, (tile_index // 2) % NZ, tile_index // (2 * NZ)
    turn = 1 - 2 * core
    own_ids = lax.dynamic_slice_in_dim(row_ids, tile_index * owned_slots, owned_slots)

    quarter = SPLIT // reps
    gathered = lax.all_gather(panel_rows[:, SPLIT:], "tiles", axis=0, tiled=True)
    own = lax.dynamic_slice_in_dim(panel_rows, rep_index * quarter, quarter, 1)
    column = [own] + [lax.ppermute(own, "tiles", y_perm(step)) for step in (1, 2, -1)]
    buffers = ring(jnp.concatenate(column, axis=0), NZ, z_perm(1), z_perm(-1))

    both_lists = lax.dynamic_slice_in_dim(membership, (tile_index // 2) * 2, 2, 0)
    match = both_lists[:, :, None] == row_ids[None, None, :]
    position = jnp.arange(row_ids.shape[0], dtype=jnp.int32)
    where = jnp.max(jnp.where(match, position[None, None, :], 0), axis=2)
    where = jnp.where(core == 0, where, where[::-1])
    slots = where[0]
    valid = (lax.dynamic_index_in_dim(membership, tile_index, 0, keepdims=False) < NB).astype(jnp.int32)
    ez = (turn * (my_z - (where // 4) % NZ)) % NZ
    ey = (turn * (my_y - where // (4 * NZ))) % NY
    place = jnp.stack([ez, ey * owned_slots + where % owned_slots], axis=1)
    here = (slots // 2) % 2 == core

    mine, theirs = pick(buffers, place)
    swap = [(t, t ^ 1) for t in range(tiles)]
    mine = jnp.where(here[:, None, None], mine, lax.ppermute(theirs, "tiles", swap))
    both = ("tiles", "rep")
    ahead, back = x_perm(tiles, reps, 1), x_perm(tiles, reps, -1)
    one = lax.ppermute(mine, both, ahead)
    other = lax.ppermute(mine, both, back)
    far = lax.ppermute(one, both, ahead)
    quarters = [(rep_index + shift + reps) % reps for shift in (0, -turn, turn, 2)]

    high, low, full_high, full_low, diag = factorize(pivot_blocks, coupling)
    factors = own_factors(panel_rows, high, low, diag, own_ids < NB)
    parts = []
    for part in (mine, one, other, far):
        parts.extend(prepare(part, full_high, full_low, valid))
    updated = update_tiles(trailing_tiles, full_high, full_low, parts, quarters, gathered, slots, valid, tile_pairs)
    return (updated, factors, diag.reshape(2, b))


def solution(mesh):
    return jax.shard_map(
        functools.partial(per_device, mesh.shape["tiles"], mesh.shape["rep"]),
        mesh=mesh,
        in_specs=(
            P(("tiles", "rep"), None, None),
            P("tiles", None, None),
            P(),
            P(),
            P(),
            P(),
            P(("tiles", "rep"), None),
        ),
        out_specs=(P(("tiles", "rep"), None, None), P("tiles", None, None), P()),
        check_vma=False,
    )
```

```python
import functools

import jax
import jax.numpy as jnp
from jax import lax
from jax.experimental import pallas as pl
from jax.experimental.pallas import tpu as pltpu
from jax.sharding import PartitionSpec as P


NB = 96
NY, NZ = 4, 8
SPLIT = 128
W = 64
GROUP = 4
F32 = jnp.float32
BF = jnp.bfloat16
HI = lax.Precision.HIGHEST


def dot(a, b):
    return lax.dot_general(a, b, (((1,), (0,)), ((), ())), precision=HI, preferred_element_type=F32)


def dot_nt(a, b):
    return lax.dot_general(a, b, (((1,), (1,)), ((), ())), precision=HI, preferred_element_type=F32)


def split(x):
    hi = x.astype(BF)
    return hi, (x - hi.astype(F32)).astype(BF)


def dot3(ah, al, bh, bl, nt=False):
    dims = (((1,), (1 if nt else 0,)), ((), ()))
    f = functools.partial(lax.dot_general, dimension_numbers=dims, preferred_element_type=F32)
    return f(ah, bh) + (f(ah, bl) + f(al, bh))


def eliminate(state, diag, at, n):
    lo, up = at * W, (at + 1) * W
    block = state[lo:up, lo:up]
    rows = lax.broadcasted_iota(jnp.int32, (W, 2 * W), 0)
    lanes = lax.broadcasted_iota(jnp.int32, (W, 2 * W), 1)
    eye = (lax.broadcasted_iota(jnp.int32, (W, W), 0) == lax.broadcasted_iota(jnp.int32, (W, W), 1))
    aug = jnp.concatenate([block, eye.astype(F32)], axis=1)
    for first in range(0, W, GROUP):
        columns = [jnp.broadcast_to(aug[:, k : k + 1], (W, 2 * W)) for k in range(first, first + GROUP)]
        for k in range(first, first + GROUP):
            column = columns[k - first]
            reciprocal = 1.0 / column[k : k + 1, :]
            below = jnp.where(rows > k, column, 0.0)
            aug = aug - below * (aug[k : k + 1, :] * reciprocal)
            for later in range(k + 1 - first, GROUP):
                columns[later] = columns[later] - below * (columns[later][k : k + 1, :] * reciprocal)
    inverse = aug[:, W:]
    on_diag = jnp.where(rows == lanes, aug, 0.0)
    d_col = jnp.sum(on_diag, axis=1, keepdims=True)
    diag[0:1, (at % 2) * W : (at % 2 + 1) * W] = jnp.sum(on_diag, axis=0, keepdims=True)[:, :W]
    width = state.shape[1]
    col = lax.broadcasted_iota(jnp.int32, (W, width), 1)
    row = lax.broadcasted_iota(jnp.int32, (W, width), 0)
    own = state[lo:up, :]
    own = jnp.where((col >= lo) & (col < up), (col - lo == row).astype(F32), own)
    if up < n:
        below = dot(dot_nt(state[up:n, lo:up], inverse), inverse / d_col)
        base = state[up:n, :]
        bcol = lax.broadcasted_iota(jnp.int32, base.shape, 1)
        base = jnp.where((bcol >= lo) & (bcol < up), 0.0, base)
        state[up:n, :] = base - dot(below, own)
    state[lo:up, :] = jnp.where(col < up, dot(inverse, own), 0.0)


def first_kernel(pivot, coupling, state, diag):
    h = coupling.shape[0]
    state[:h, :h] = pivot[0]
    state[h:, :h] = coupling[...]
    state[:h, h:] = coupling[...].T
    state[h:, h:] = pivot[1]
    for at in (0, 1):
        eliminate(state, diag, at, 2 * h)


def middle_kernel(at, before, state, diag):
    state[...] = before[...]
    for p in (at, at + 1):
        eliminate(state, diag, p, state.shape[0])


def last_kernel(at, before, d0, d1, d2, high, low, full_high, full_low, diag, state, last):
    state[...] = before[...]
    for p in (at, at + 1):
        eliminate(state, last, p, state.shape[0])
    for p, d in enumerate((d0, d1, d2, last)):
        diag[0:1, p * 2 * W : (p + 1) * 2 * W] = d[...]
    inverse = state[...]
    turned = inverse.T
    high[...], low[...] = split(turned)
    full_high[...], full_low[...] = split(dot(turned / diag[...], inverse))


def cost(flops, nbytes):
    return pl.CostEstimate(flops=int(flops), bytes_accessed=int(nbytes), transcendentals=0)


def factorize(pivot_blocks, coupling):
    n = 2 * coupling.shape[0]
    full = jax.ShapeDtypeStruct((n, n), F32)
    half = jax.ShapeDtypeStruct((n, n), BF)
    dshape = jax.ShapeDtypeStruct((1, 2 * W), F32)
    work = cost(6e9, 2 * n * n * 4)
    diags = []
    state, d = pl.pallas_call(first_kernel, out_shape=(full, dshape), cost_estimate=work, name="panels0")(pivot_blocks, coupling)
    diags.append(d)
    for at in (2, 4):
        state, d = pl.pallas_call(
            functools.partial(middle_kernel, at), out_shape=(full, dshape), cost_estimate=work
        )(state)
        diags.append(d)
    return pl.pallas_call(
        functools.partial(last_kernel, 6),
        out_shape=(half, half, half, half, jax.ShapeDtypeStruct((1, n), F32)),
        scratch_shapes=[pltpu.VMEM((n, n), F32), pltpu.VMEM((1, 2 * W), F32)],
        cost_estimate=work,
        name="panels6",
    )(state, *diags)


def apply_inverse(x, high, low):
    h = high.shape[0] // 2
    xh, xl = split(x)
    first = dot3(xh[:, :h], xl[:, :h], high[:h, :h], low[:h, :h])
    second = dot3(xh, xl, high[:, h:], low[:, h:])
    return jnp.concatenate([first, second], axis=1)


def own_kernel(keep, x, high, low, diag, out):
    i = pl.program_id(0)
    rows = x.shape[1] // 4

    @pl.loop(0, 4)
    def _(part):
        at = pl.ds(pl.multiple_of(part * rows, rows), rows)
        y = apply_inverse(x[0, at], high, low) / diag[...]
        out[0, at] = jnp.where(keep[i] > 0, y, 0.0)


def own_factors(panel_rows, high, low, diag, usable):
    slots, b, n = panel_rows.shape
    const = lambda i, k: (0, 0)
    return pl.pallas_call(
        own_kernel,
        out_shape=jax.ShapeDtypeStruct(panel_rows.shape, F32),
        grid_spec=pltpu.PrefetchScalarGridSpec(
            num_scalar_prefetch=1,
            grid=(slots,),
            in_specs=[
                pl.BlockSpec((1, b, n), lambda i, k: (i, 0, 0)),
                pl.BlockSpec((n, n), const),
                pl.BlockSpec((n, n), const),
                pl.BlockSpec((1, n), const),
            ],
            out_specs=pl.BlockSpec((1, b, n), lambda i, k: (i, 0, 0)),
        ),
        cost_estimate=cost(slots * b * n * n * 6, slots * b * n * 8),
        name="own_factors",
    )(usable.astype(jnp.int32), panel_rows, high, low, diag)


def pick_kernel(place, *refs):
    nz, ny = 8, 4
    zy = refs[:nz]
    yz = refs[nz : nz + ny]
    outs = refs[nz + ny : nz + ny + 2]
    sems = refs[nz + ny + 2]
    count, rows, _ = outs[0].shape
    half = rows // 2

    def copy(color, which, g, source, at):
        target = outs[which].at[g, pl.ds(color * half, half)]
        return pltpu.make_async_copy(source.at[at], target, sems.at[color, which, g])

    for which in range(2):

        @pl.loop(0, count)
        def _(g):
            ez, ey, slot = place[which, 0, g], place[which, 1, g], place[which, 2, g]
            for e in range(nz):

                @pl.when(ez == e)
                def _():
                    copy(0, which, g, zy[e], ey * 2 + slot).start()

            for e in range(ny):

                @pl.when(ey == e)
                def _():
                    copy(1, which, g, yz[e], ez * 2 + slot).start()

    for which in range(2):

        @pl.loop(0, count)
        def _(g):
            copy(0, which, g, zy[0], 0).wait()
            copy(1, which, g, yz[0], 0).wait()


def pick(zy, yz, place, rows, n):
    count = place.shape[2]
    shape = jax.ShapeDtypeStruct((count, rows, n), F32)
    return pl.pallas_call(
        pick_kernel,
        out_shape=(shape, shape),
        grid_spec=pltpu.PrefetchScalarGridSpec(
            num_scalar_prefetch=1,
            grid=(),
            in_specs=[pl.BlockSpec(memory_space=pl.ANY)] * (len(zy) + len(yz)),
            out_specs=(pl.BlockSpec(memory_space=pltpu.VMEM),) * 2,
            scratch_shapes=[pltpu.SemaphoreType.DMA((2, 2, count))],
        ),
        cost_estimate=cost(0, 4 * 4 * count * rows * n),
        name="pick",
    )(place, *zy, *yz)


def prepare_kernel(valid, x, full_high, full_low, high, low):
    count, rows, n = x.shape
    half = count // 2
    step = 4

    @pl.loop(0, half // step)
    def _(i):
        at = i * step
        part = jnp.stack([jnp.where(valid[at + g] > 0, x[at + g], 0.0) for g in range(step)])
        xh, xl = split(part.reshape(step * rows, n))
        yh, yl = split(dot3(xh, xl, full_high[...], full_low[...]))
        high[pl.ds(at, step)] = yh.reshape(step, rows, n)
        low[pl.ds(at, step)] = yl.reshape(step, rows, n)

    @pl.loop(half, count)
    def _(g):
        xh, xl = split(jnp.where(valid[g] > 0, x[g], 0.0))
        high[g] = xh
        low[g] = xl


def prepare(x, full_high, full_low, valid):
    count, rows, n = x.shape
    shape = jax.ShapeDtypeStruct(x.shape, BF)
    vmem = pl.BlockSpec(memory_space=pltpu.VMEM)
    return pl.pallas_call(
        prepare_kernel,
        out_shape=(shape, shape),
        grid_spec=pltpu.PrefetchScalarGridSpec(
            num_scalar_prefetch=1, grid=(), in_specs=[vmem] * 3, out_specs=(vmem, vmem)
        ),
        cost_estimate=cost(count // 2 * rows * n * n * 6, count * rows * n * 8),
        name="prepare",
    )(valid, x, full_high, full_low)


def update_kernel(info, tile, full_high, full_low, *refs):
    parts, (table, out, stage, lh, ll, rh, rl, sems) = refs[:8], refs[8:]
    k = pl.program_id(0)
    count, tail, _ = stage.shape
    half, b, _ = lh.shape
    rows = parts[0].shape[1]
    head = b - tail
    step = 2

    @pl.when(k == 0)
    def _():
        def rest(g):
            return pltpu.make_async_copy(table.at[info[4, g]], stage.at[g], sems.at[g])

        @pl.loop(0, count)
        def _(g):
            rest(g).start()

        placed = []
        for i in range(8):
            at = pl.ds(pl.multiple_of(info[3, i // 2] * rows, rows), rows)
            left, right = ((lh, rh), (ll, rl))[i % 2]
            for side, target in enumerate((left, right)):
                source = parts[i].at[pl.ds(side * half, half)]
                placed.append(pltpu.make_async_copy(source, target.at[:, at, :], sems.at[count + 2 * i + side]))
        for c in placed:
            c.start()

        @pl.loop(0, half // step)
        def _(i):
            both = []
            for g in range(step):
                rest(i * step + g).wait()
                both.append(jnp.where(info[5, i * step + g] > 0, stage[i * step + g], 0.0))
            xh, xl = split(jnp.concatenate(both, axis=0))
            yh, yl = split(dot3(xh, xl, full_high[...], full_low[...]))
            for g in range(step):
                lh[i * step + g, head:] = yh[g * tail : (g + 1) * tail]
                ll[i * step + g, head:] = yl[g * tail : (g + 1) * tail]

        @pl.loop(half, count)
        def _(g):
            rest(g).wait()
            xh, xl = split(jnp.where(info[5, g] > 0, stage[g], 0.0))
            rh[g - half, head:] = xh
            rl[g - half, head:] = xl

        for c in placed:
            c.wait()

    @pl.loop(0, tile.shape[0])
    def _(t):
        slot = k * tile.shape[0] + t
        live = info[2, slot] > 0

        @pl.when(live)
        def _():
            i, j = info[0, slot], info[1, slot]
            out[t] = tile[t] - dot3(lh[i], ll[i], rh[j], rl[j], nt=True)

        @pl.when(jnp.logical_not(live))
        def _():
            out[t] = tile[t]


def update_tiles(tiles, full_high, full_low, parts, quarters, table, slots, valid, pairs):
    total, b, _ = tiles.shape
    count = slots.shape[0]
    half = count // 2
    n = full_high.shape[0]
    tail = table.shape[1]
    widest = max(total, count)
    fit = lambda v: jnp.pad(v.astype(jnp.int32), (0, widest - v.shape[0]))
    info = jnp.stack(
        [
            fit(jnp.minimum(pairs[:, 0], half - 1)),
            fit(jnp.clip(pairs[:, 1] - half, 0, half - 1)),
            fit(pairs[:, 0] < count),
            fit(jnp.stack(quarters)),
            fit(slots),
            fit(valid),
        ]
    )
    block = 4 if total % 4 == 0 else 1
    tspec = pl.BlockSpec((block, b, b), lambda k, s: (k, 0, 0))
    whole = pl.BlockSpec((n, n), lambda k, s: (0, 0))
    operand = pltpu.VMEM((half, b, n), BF)
    return pl.pallas_call(
        update_kernel,
        out_shape=jax.ShapeDtypeStruct(tiles.shape, F32),
        grid_spec=pltpu.PrefetchScalarGridSpec(
            num_scalar_prefetch=1,
            grid=(total // block,),
            in_specs=[tspec, whole, whole] + [pl.BlockSpec(memory_space=pl.ANY)] * (len(parts) + 1),
            out_specs=tspec,
            scratch_shapes=[pltpu.VMEM((count, tail, n), F32)]
            + [operand] * 4
            + [pltpu.SemaphoreType.DMA((count + 2 * len(parts),))],
        ),
        compiler_params=pltpu.CompilerParams(vmem_limit_bytes=58 * 2**20),
        cost_estimate=cost(total * b * b * n * 6 + half * tail * n * n * 6, total * b * 8 * b + count * tail * n * 4),
        name="update_tiles",
    )(info, tiles, full_high, full_low, *parts, table)


def turned(core, step):
    return step if core == 0 else -step


def tile_of(y, z, core):
    return ((y % NY) * NZ + z % NZ) * 2 + core


def chips():
    return [(y, z, c) for y in range(NY) for z in range(NZ) for c in range(2)]


def z_perm(step):
    return [(tile_of(y, z, c), tile_of(y, z + turned(c, step), c)) for y, z, c in chips()]


def y_perm(step):
    return [(tile_of(y, z, c), tile_of(y + turned(c, step), z, c)) for y, z, c in chips()]


def x_perm(tiles, reps, step):
    return [(t * reps + x, t * reps + (x + turned(t % 2, step)) % reps) for t in range(tiles) for x in range(reps)]


def ring(block, size, ahead, back):
    near, far = [block], [block]
    for k in range(size // 2):
        near.append(lax.ppermute(near[-1], "tiles", ahead))
        if k < size // 2 - 1:
            far.append(lax.ppermute(far[-1], "tiles", back))
    return near + far[:0:-1]


def per_device(tiles, reps, trailing_tiles, panel_rows, pivot_blocks, coupling, row_ids, membership, tile_pairs):
    owned_slots, b, n = panel_rows.shape
    tile_index = lax.axis_index("tiles")
    rep_index = lax.axis_index("rep")
    core, my_z, my_y = tile_index % 2, (tile_index // 2) % NZ, tile_index // (2 * NZ)
    turn = 1 - 2 * core
    own_ids = lax.dynamic_slice_in_dim(row_ids, tile_index * owned_slots, owned_slots)

    quarter = SPLIT // reps
    gathered = lax.all_gather(panel_rows[:, SPLIT:], "tiles", axis=0, tiled=True)
    half = quarter // 2
    top = lax.dynamic_slice_in_dim(panel_rows, rep_index * quarter, half, 1)
    low_rows = lax.dynamic_slice_in_dim(panel_rows, rep_index * quarter + half, half, 1)
    za, zb, ya, yb = z_perm(1), z_perm(-1), y_perm(1), y_perm(-1)
    zy = ring(jnp.concatenate(ring(top, NY, ya, yb), axis=0), NZ, za, zb)
    yz = ring(jnp.concatenate(ring(low_rows, NZ, za, zb), axis=0), NY, ya, yb)

    both_lists = lax.dynamic_slice_in_dim(membership, (tile_index // 2) * 2, 2, 0)
    match = both_lists[:, :, None] == row_ids[None, None, :]
    position = jnp.arange(row_ids.shape[0], dtype=jnp.int32)
    where = jnp.max(jnp.where(match, position[None, None, :], 0), axis=2)
    where = jnp.where(core == 0, where, where[::-1])
    slots = where[0]
    valid = (lax.dynamic_index_in_dim(membership, tile_index, 0, keepdims=False) < NB).astype(jnp.int32)
    ez = (turn * (my_z - (where // 4) % NZ)) % NZ
    ey = (turn * (my_y - where // (4 * NZ))) % NY
    place = jnp.stack([ez, ey, where % owned_slots], axis=1)
    here = (slots // 2) % 2 == core

    mine, theirs = pick(zy, yz, place, quarter, n)
    swap = [(t, t ^ 1) for t in range(tiles)]
    mine = jnp.where(here[:, None, None], mine, lax.ppermute(theirs, "tiles", swap))
    both = ("tiles", "rep")
    ahead, back = x_perm(tiles, reps, 1), x_perm(tiles, reps, -1)
    one = lax.ppermute(mine, both, ahead)
    other = lax.ppermute(mine, both, back)
    far = lax.ppermute(one, both, ahead)
    quarters = [(rep_index + shift + reps) % reps for shift in (0, -turn, turn, 2)]

    high, low, full_high, full_low, diag = factorize(pivot_blocks, coupling)
    factors = own_factors(panel_rows, high, low, diag, own_ids < NB)
    parts = []
    for part in (mine, one, other, far):
        parts.extend(prepare(part, full_high, full_low, valid))
    updated = update_tiles(trailing_tiles, full_high, full_low, parts, quarters, gathered, slots, valid, tile_pairs)
    return (updated, factors, diag.reshape(2, b))


def solution(mesh):
    return jax.shard_map(
        functools.partial(per_device, mesh.shape["tiles"], mesh.shape["rep"]),
        mesh=mesh,
        in_specs=(
            P(("tiles", "rep"), None, None),
            P("tiles", None, None),
            P(),
            P(),
            P(),
            P(),
            P(("tiles", "rep"), None),
        ),
        out_specs=(P(("tiles", "rep"), None, None), P("tiles", None, None), P()),
        check_vma=False,
    )
```

```python
import functools

import jax
import jax.numpy as jnp
from jax import lax
from jax.experimental import pallas as pl
from jax.experimental.pallas import tpu as pltpu
from jax.sharding import PartitionSpec as P


NB = 96
NY, NZ = 4, 8
SPLIT = 128
W = 64
GROUP = 4
F32 = jnp.float32
BF = jnp.bfloat16
HI = lax.Precision.HIGHEST


def dot(a, b):
    return lax.dot_general(a, b, (((1,), (0,)), ((), ())), precision=HI, preferred_element_type=F32)


def dot_nt(a, b):
    return lax.dot_general(a, b, (((1,), (1,)), ((), ())), precision=HI, preferred_element_type=F32)


def split(x):
    hi = x.astype(BF)
    return hi, (x - hi.astype(F32)).astype(BF)


def dot3(ah, al, bh, bl, nt=False):
    dims = (((1,), (1 if nt else 0,)), ((), ()))
    f = functools.partial(lax.dot_general, dimension_numbers=dims, preferred_element_type=F32)
    return f(ah, bh) + (f(ah, bl) + f(al, bh))


def load_panel(state, work, at):
    lo, up = at * W, (at + 1) * W
    eye = lax.broadcasted_iota(jnp.int32, (W, W), 0) == lax.broadcasted_iota(jnp.int32, (W, W), 1)
    work[...] = jnp.concatenate([state[lo:up, lo:up], eye.astype(F32)], axis=1)


def pivot_steps(work):
    rows = lax.broadcasted_iota(jnp.int32, (W, 2 * W), 0)
    aug = work[...]
    for first in range(0, W, GROUP):
        columns = [jnp.broadcast_to(aug[:, k : k + 1], (W, 2 * W)) for k in range(first, first + GROUP)]
        for k in range(first, first + GROUP):
            column = columns[k - first]
            reciprocal = 1.0 / column[k : k + 1, :]
            below = jnp.where(rows > k, column, 0.0)
            aug = aug - below * (aug[k : k + 1, :] * reciprocal)
            for later in range(k + 1 - first, GROUP):
                columns[later] = columns[later] - below * (columns[later][k : k + 1, :] * reciprocal)
    work[...] = aug


def finish_panel(state, work, diag, at, n):
    lo, up = at * W, (at + 1) * W
    rows = lax.broadcasted_iota(jnp.int32, (W, 2 * W), 0)
    lanes = lax.broadcasted_iota(jnp.int32, (W, 2 * W), 1)
    aug = work[...]
    inverse = aug[:, W:]
    on_diag = jnp.where(rows == lanes, aug, 0.0)
    d_col = jnp.sum(on_diag, axis=1, keepdims=True)
    diag[0:1, (at % 2) * W : (at % 2 + 1) * W] = jnp.sum(on_diag, axis=0, keepdims=True)[:, :W]
    width = state.shape[1]
    col = lax.broadcasted_iota(jnp.int32, (W, width), 1)
    row = lax.broadcasted_iota(jnp.int32, (W, width), 0)
    own = jnp.where((col >= lo) & (col < up), (col - lo == row).astype(F32), state[lo:up, :])
    if up < n:
        below = dot(dot_nt(state[up:n, lo:up], inverse), inverse / d_col)
        base = state[up:n, :]
        bcol = lax.broadcasted_iota(jnp.int32, base.shape, 1)
        base = jnp.where((bcol >= lo) & (bcol < up), 0.0, base)
        state[up:n, :] = base - dot(below, own)
    state[lo:up, :] = jnp.where(col < up, dot(inverse, own), 0.0)


def eliminate(state, diag, work, at):
    @pl.loop(0, 2)
    def _(i):
        for p in range(2):

            @pl.when(i == p)
            def _():
                load_panel(state, work, at + p)

        pivot_steps(work)
        for p in range(2):

            @pl.when(i == p)
            def _():
                finish_panel(state, work, diag, at + p, state.shape[0])


def first_kernel(pivot, coupling, state, diag, work):
    h = coupling.shape[0]
    state[:h, :h] = pivot[0]
    state[h:, :h] = coupling[...]
    state[:h, h:] = coupling[...].T
    state[h:, h:] = pivot[1]
    eliminate(state, diag, work, 0)


def middle_kernel(at, before, state, diag, work):
    state[...] = before[...]
    eliminate(state, diag, work, at)


def last_kernel(at, before, d0, d1, d2, high, low, full_high, full_low, diag, state, last, scaled, work):
    state[...] = before[...]
    eliminate(state, last, work, at)
    for p, d in enumerate((d0, d1, d2, last)):
        diag[0:1, p * 2 * W : (p + 1) * 2 * W] = d[...]
    turned = state[...].T
    high[...], low[...] = split(turned)
    scaled[...] = turned / diag[...]
    step = 2 * W

    @pl.loop(0, state.shape[0] // step)
    def _(i):
        at = pl.ds(pl.multiple_of(i * step, step), step)
        full_high[at, :], full_low[at, :] = split(dot(scaled[at, :], state[...]))


def cost(flops, nbytes):
    return pl.CostEstimate(flops=int(flops), bytes_accessed=int(nbytes), transcendentals=0)


def factorize(pivot_blocks, coupling):
    n = 2 * coupling.shape[0]
    full = jax.ShapeDtypeStruct((n, n), F32)
    half = jax.ShapeDtypeStruct((n, n), BF)
    dshape = jax.ShapeDtypeStruct((1, 2 * W), F32)
    work = cost(6e9, 2 * n * n * 4)
    diags = []
    panel = pltpu.VMEM((W, 2 * W), F32)
    state, d = pl.pallas_call(
        first_kernel, out_shape=(full, dshape), scratch_shapes=[panel], cost_estimate=work, name="panels0"
    )(pivot_blocks, coupling)
    diags.append(d)
    for at in (2, 4):
        state, d = pl.pallas_call(
            functools.partial(middle_kernel, at), out_shape=(full, dshape), scratch_shapes=[panel], cost_estimate=work
        )(state)
        diags.append(d)
    return pl.pallas_call(
        functools.partial(last_kernel, 6),
        out_shape=(half, half, half, half, jax.ShapeDtypeStruct((1, n), F32)),
        scratch_shapes=[pltpu.VMEM((n, n), F32), pltpu.VMEM((1, 2 * W), F32), pltpu.VMEM((n, n), F32), panel],
        cost_estimate=work,
        name="panels6",
    )(state, *diags)


def apply_inverse(x, high, low):
    h = high.shape[0] // 2
    xh, xl = split(x)
    first = dot3(xh[:, :h], xl[:, :h], high[:h, :h], low[:h, :h])
    second = dot3(xh, xl, high[:, h:], low[:, h:])
    return jnp.concatenate([first, second], axis=1)


def own_kernel(keep, x, high, low, diag, out):
    i = pl.program_id(0)
    y = apply_inverse(x[0], high, low) / diag[...]
    out[0] = jnp.where(keep[i] > 0, y, 0.0)


def own_factors(panel_rows, high, low, diag, usable):
    slots, b, n = panel_rows.shape
    const = lambda i, k: (0, 0)
    return pl.pallas_call(
        own_kernel,
        out_shape=jax.ShapeDtypeStruct(panel_rows.shape, F32),
        grid_spec=pltpu.PrefetchScalarGridSpec(
            num_scalar_prefetch=1,
            grid=(slots,),
            in_specs=[
                pl.BlockSpec((1, b, n), lambda i, k: (i, 0, 0)),
                pl.BlockSpec((n, n), const),
                pl.BlockSpec((n, n), const),
                pl.BlockSpec((1, n), const),
            ],
            out_specs=pl.BlockSpec((1, b, n), lambda i, k: (i, 0, 0)),
        ),
        cost_estimate=cost(slots * b * n * n * 6, slots * b * n * 8),
        name="own_factors",
    )(usable.astype(jnp.int32), panel_rows, high, low, diag)


def pick_kernel(place, *refs):
    nz, ny = 8, 4
    zy = refs[:nz]
    yz = refs[nz : nz + ny]
    outs = refs[nz + ny : nz + ny + 2]
    sems = refs[nz + ny + 2]
    count, rows, _ = outs[0].shape
    half = rows // 2

    def copy(color, which, g, source, at):
        target = outs[which].at[g, pl.ds(color * half, half)]
        return pltpu.make_async_copy(source.at[at], target, sems.at[color, which, g])

    for which in range(2):

        @pl.loop(0, count)
        def _(g):
            ez, ey, slot = place[which, 0, g], place[which, 1, g], place[which, 2, g]
            for e in range(nz):

                @pl.when(ez == e)
                def _():
                    copy(0, which, g, zy[e], ey * 2 + slot).start()

            for e in range(ny):

                @pl.when(ey == e)
                def _():
                    copy(1, which, g, yz[e], ez * 2 + slot).start()

    for which in range(2):

        @pl.loop(0, count)
        def _(g):
            copy(0, which, g, zy[0], 0).wait()
            copy(1, which, g, yz[0], 0).wait()


def pick(zy, yz, place, rows, n):
    count = place.shape[2]
    shape = jax.ShapeDtypeStruct((count, rows, n), F32)
    return pl.pallas_call(
        pick_kernel,
        out_shape=(shape, shape),
        grid_spec=pltpu.PrefetchScalarGridSpec(
            num_scalar_prefetch=1,
            grid=(),
            in_specs=[pl.BlockSpec(memory_space=pl.ANY)] * (len(zy) + len(yz)),
            out_specs=(pl.BlockSpec(memory_space=pltpu.VMEM),) * 2,
            scratch_shapes=[pltpu.SemaphoreType.DMA((2, 2, count))],
        ),
        cost_estimate=cost(0, 4 * 4 * count * rows * n),
        name="pick",
    )(place, *zy, *yz)


def update_kernel(info, tile, full_high, full_low, p0, p1, p2, p3, table, out, stage, lh, ll, rh, rl, sems):
    k = pl.program_id(0)
    count, b, _ = stage.shape
    half = count // 2
    rows = p0.shape[1]
    tail = table.shape[1]

    @pl.when(k == 0)
    def _():
        parts = [
            pltpu.make_async_copy(p, stage.at[:, pl.ds(pl.multiple_of(info[3, i] * rows, rows), rows), :], sems.at[count + i])
            for i, p in enumerate((p0, p1, p2, p3))
        ]
        for c in parts:
            c.start()

        def rest(g):
            return pltpu.make_async_copy(table.at[info[4, g]], stage.at[g, pl.ds(b - tail, tail), :], sems.at[g])

        @pl.loop(0, count)
        def _(g):
            rest(g).start()

        for c in parts:
            c.wait()

        @pl.loop(0, half)
        def _(g):
            rest(g).wait()
            x = jnp.where(info[5, g] > 0, stage[g], 0.0)
            xh, xl = split(x)
            yh, yl = split(dot3(xh, xl, full_high[...], full_low[...]))
            lh[g] = yh
            ll[g] = yl

        @pl.loop(half, count)
        def _(g):
            rest(g).wait()
            x = jnp.where(info[5, g] > 0, stage[g], 0.0)
            xh, xl = split(x)
            rh[g - half] = xh
            rl[g - half] = xl

    @pl.loop(0, tile.shape[0])
    def _(t):
        slot = k * tile.shape[0] + t
        live = info[2, slot] > 0

        @pl.when(live)
        def _():
            i, j = info[0, slot], info[1, slot]
            out[t] = tile[t] - dot3(lh[i], ll[i], rh[j], rl[j], nt=True)

        @pl.when(jnp.logical_not(live))
        def _():
            out[t] = tile[t]


def update_tiles(tiles, full_high, full_low, parts, quarters, table, slots, valid, pairs):
    total, b, _ = tiles.shape
    count = slots.shape[0]
    half = count // 2
    n = full_high.shape[0]
    widest = max(total, count)
    fit = lambda v: jnp.pad(v.astype(jnp.int32), (0, widest - v.shape[0]))
    info = jnp.stack(
        [
            fit(jnp.minimum(pairs[:, 0], half - 1)),
            fit(jnp.clip(pairs[:, 1] - half, 0, half - 1)),
            fit(pairs[:, 0] < count),
            fit(jnp.stack(quarters)),
            fit(slots),
            fit(valid),
        ]
    )
    block = 4 if total % 4 == 0 else 1
    tspec = pl.BlockSpec((block, b, b), lambda k, s: (k, 0, 0))
    whole = pl.BlockSpec((n, n), lambda k, s: (0, 0))
    anywhere = pl.BlockSpec(memory_space=pl.ANY)
    operand = pltpu.VMEM((half, b, n), BF)
    return pl.pallas_call(
        update_kernel,
        out_shape=jax.ShapeDtypeStruct(tiles.shape, F32),
        grid_spec=pltpu.PrefetchScalarGridSpec(
            num_scalar_prefetch=1,
            grid=(total // block,),
            in_specs=[tspec, whole, whole] + [anywhere] * 5,
            out_specs=tspec,
            scratch_shapes=[pltpu.VMEM((count, b, n), F32)]
            + [operand] * 4
            + [pltpu.SemaphoreType.DMA((count + 4,))],
        ),
        compiler_params=pltpu.CompilerParams(vmem_limit_bytes=58 * 2**20),
        cost_estimate=cost(total * b * b * n * 6 + half * b * n * n * 6, total * b * 8 * b + count * b * n * 4),
        name="update_tiles",
    )(info, tiles, full_high, full_low, *parts, table)


def turned(core, step):
    return step if core == 0 else -step


def tile_of(y, z, core):
    return ((y % NY) * NZ + z % NZ) * 2 + core


def chips():
    return [(y, z, c) for y in range(NY) for z in range(NZ) for c in range(2)]


def z_perm(step):
    return [(tile_of(y, z, c), tile_of(y, z + turned(c, step), c)) for y, z, c in chips()]


def y_perm(step):
    return [(tile_of(y, z, c), tile_of(y + turned(c, step), z, c)) for y, z, c in chips()]


def x_perm(tiles, reps, step):
    return [(t * reps + x, t * reps + (x + turned(t % 2, step)) % reps) for t in range(tiles) for x in range(reps)]


def ring(block, size, ahead, back):
    near, far = [block], [block]
    for k in range(size // 2):
        near.append(lax.ppermute(near[-1], "tiles", ahead))
        if k < size // 2 - 1:
            far.append(lax.ppermute(far[-1], "tiles", back))
    return near + far[:0:-1]


def per_device(tiles, reps, trailing_tiles, panel_rows, pivot_blocks, coupling, row_ids, membership, tile_pairs):
    owned_slots, b, n = panel_rows.shape
    tile_index = lax.axis_index("tiles")
    rep_index = lax.axis_index("rep")
    core, my_z, my_y = tile_index % 2, (tile_index // 2) % NZ, tile_index // (2 * NZ)
    turn = 1 - 2 * core
    own_ids = lax.dynamic_slice_in_dim(row_ids, tile_index * owned_slots, owned_slots)

    quarter = SPLIT // reps
    gathered = lax.all_gather(panel_rows[:, SPLIT:], "tiles", axis=0, tiled=True)
    half = quarter // 2
    top = lax.dynamic_slice_in_dim(panel_rows, rep_index * quarter, half, 1)
    low_rows = lax.dynamic_slice_in_dim(panel_rows, rep_index * quarter + half, half, 1)
    za, zb, ya, yb = z_perm(1), z_perm(-1), y_perm(1), y_perm(-1)
    zy = ring(jnp.concatenate(ring(top, NY, ya, yb), axis=0), NZ, za, zb)
    yz = ring(jnp.concatenate(ring(low_rows, NZ, za, zb), axis=0), NY, ya, yb)

    both_lists = lax.dynamic_slice_in_dim(membership, (tile_index // 2) * 2, 2, 0)
    match = both_lists[:, :, None] == row_ids[None, None, :]
    position = jnp.arange(row_ids.shape[0], dtype=jnp.int32)
    where = jnp.max(jnp.where(match, position[None, None, :], 0), axis=2)
    where = jnp.where(core == 0, where, where[::-1])
    slots = where[0]
    valid = (lax.dynamic_index_in_dim(membership, tile_index, 0, keepdims=False) < NB).astype(jnp.int32)
    ez = (turn * (my_z - (where // 4) % NZ)) % NZ
    ey = (turn * (my_y - where // (4 * NZ))) % NY
    place = jnp.stack([ez, ey, where % owned_slots], axis=1)
    here = (slots // 2) % 2 == core

    mine, theirs = pick(zy, yz, place, quarter, n)
    swap = [(t, t ^ 1) for t in range(tiles)]
    mine = jnp.where(here[:, None, None], mine, lax.ppermute(theirs, "tiles", swap))
    both = ("tiles", "rep")
    ahead, back = x_perm(tiles, reps, 1), x_perm(tiles, reps, -1)
    one = lax.ppermute(mine, both, ahead)
    other = lax.ppermute(mine, both, back)
    far = lax.ppermute(one, both, ahead)
    quarters = [(rep_index + shift + reps) % reps for shift in (0, -turn, turn, 2)]

    high, low, full_high, full_low, diag = factorize(pivot_blocks, coupling)
    factors = own_factors(panel_rows, high, low, diag, own_ids < NB)
    parts = (mine, one, other, far)
    updated = update_tiles(trailing_tiles, full_high, full_low, parts, quarters, gathered, slots, valid, tile_pairs)
    return (updated, factors, diag.reshape(2, b))


def solution(mesh):
    return jax.shard_map(
        functools.partial(per_device, mesh.shape["tiles"], mesh.shape["rep"]),
        mesh=mesh,
        in_specs=(
            P(("tiles", "rep"), None, None),
            P("tiles", None, None),
            P(),
            P(),
            P(),
            P(),
            P(("tiles", "rep"), None),
        ),
        out_specs=(P(("tiles", "rep"), None, None), P("tiles", None, None), P()),
        check_vma=False,
    )
```

```python
import functools

import jax
import jax.numpy as jnp
from jax import lax
from jax.experimental import pallas as pl
from jax.experimental.pallas import tpu as pltpu
from jax.sharding import PartitionSpec as P


NB = 96
NY, NZ = 4, 8
SPLIT = 128
W = 64
GROUP = 4
F32 = jnp.float32
BF = jnp.bfloat16
HI = lax.Precision.HIGHEST


def dot(a, b):
    return lax.dot_general(a, b, (((1,), (0,)), ((), ())), precision=HI, preferred_element_type=F32)


def dot_nt(a, b):
    return lax.dot_general(a, b, (((1,), (1,)), ((), ())), precision=HI, preferred_element_type=F32)


def split(x):
    hi = x.astype(BF)
    return hi, (x - hi.astype(F32)).astype(BF)


def dot3(ah, al, bh, bl, nt=False):
    dims = (((1,), (1 if nt else 0,)), ((), ()))
    f = functools.partial(lax.dot_general, dimension_numbers=dims, preferred_element_type=F32)
    return f(ah, bh) + (f(ah, bl) + f(al, bh))


def load_panel(state, work, at):
    lo, up = at * W, (at + 1) * W
    eye = lax.broadcasted_iota(jnp.int32, (W, W), 0) == lax.broadcasted_iota(jnp.int32, (W, W), 1)
    work[...] = jnp.concatenate([state[lo:up, lo:up], eye.astype(F32)], axis=1)


def pivot_steps(work):
    rows = lax.broadcasted_iota(jnp.int32, (W, 2 * W), 0)
    aug = work[...]
    for first in range(0, W, GROUP):
        columns = [jnp.broadcast_to(aug[:, k : k + 1], (W, 2 * W)) for k in range(first, first + GROUP)]
        for k in range(first, first + GROUP):
            column = columns[k - first]
            reciprocal = 1.0 / column[k : k + 1, :]
            below = jnp.where(rows > k, column, 0.0)
            aug = aug - below * (aug[k : k + 1, :] * reciprocal)
            for later in range(k + 1 - first, GROUP):
                columns[later] = columns[later] - below * (columns[later][k : k + 1, :] * reciprocal)
    work[...] = aug


def finish_panel(state, work, diag, at, n):
    lo, up = at * W, (at + 1) * W
    rows = lax.broadcasted_iota(jnp.int32, (W, 2 * W), 0)
    lanes = lax.broadcasted_iota(jnp.int32, (W, 2 * W), 1)
    aug = work[...]
    inverse = aug[:, W:]
    on_diag = jnp.where(rows == lanes, aug, 0.0)
    d_col = jnp.sum(on_diag, axis=1, keepdims=True)
    diag[0:1, (at % 2) * W : (at % 2 + 1) * W] = jnp.sum(on_diag, axis=0, keepdims=True)[:, :W]
    width = state.shape[1]
    col = lax.broadcasted_iota(jnp.int32, (W, width), 1)
    row = lax.broadcasted_iota(jnp.int32, (W, width), 0)
    own = jnp.where((col >= lo) & (col < up), (col - lo == row).astype(F32), state[lo:up, :])
    if up < n:
        below = dot(dot_nt(state[up:n, lo:up], inverse), inverse / d_col)
        base = state[up:n, :]
        bcol = lax.broadcasted_iota(jnp.int32, base.shape, 1)
        base = jnp.where((bcol >= lo) & (bcol < up), 0.0, base)
        state[up:n, :] = base - dot(below, own)
    state[lo:up, :] = jnp.where(col < up, dot(inverse, own), 0.0)


def eliminate(state, diag, work, at):
    @pl.loop(0, 2)
    def _(i):
        for p in range(2):

            @pl.when(i == p)
            def _():
                load_panel(state, work, at + p)

        pivot_steps(work)
        for p in range(2):

            @pl.when(i == p)
            def _():
                finish_panel(state, work, diag, at + p, state.shape[0])


def first_kernel(pivot, coupling, state, diag, work):
    h = coupling.shape[0]
    state[:h, :h] = pivot[0]
    state[h:, :h] = coupling[...]
    state[:h, h:] = coupling[...].T
    state[h:, h:] = pivot[1]
    eliminate(state, diag, work, 0)


def middle_kernel(at, before, state, diag, work):
    state[...] = before[...]
    eliminate(state, diag, work, at)


def last_kernel(at, before, d0, d1, d2, high, low, full_high, full_low, diag, state, last, scaled, work):
    state[...] = before[...]
    eliminate(state, last, work, at)
    for p, d in enumerate((d0, d1, d2, last)):
        diag[0:1, p * 2 * W : (p + 1) * 2 * W] = d[...]
    turned = state[...].T
    high[...], low[...] = split(turned)
    scaled[...] = turned / diag[...]
    step = 2 * W

    @pl.loop(0, state.shape[0] // step)
    def _(i):
        at = pl.ds(pl.multiple_of(i * step, step), step)
        full_high[at, :], full_low[at, :] = split(dot(scaled[at, :], state[...]))


def cost(flops, nbytes):
    return pl.CostEstimate(flops=int(flops), bytes_accessed=int(nbytes), transcendentals=0)


def factorize(pivot_blocks, coupling):
    n = 2 * coupling.shape[0]
    full = jax.ShapeDtypeStruct((n, n), F32)
    half = jax.ShapeDtypeStruct((n, n), BF)
    dshape = jax.ShapeDtypeStruct((1, 2 * W), F32)
    work = cost(6e9, 2 * n * n * 4)
    diags = []
    panel = pltpu.VMEM((W, 2 * W), F32)
    state, d = pl.pallas_call(
        first_kernel, out_shape=(full, dshape), scratch_shapes=[panel], cost_estimate=work, name="panels0"
    )(pivot_blocks, coupling)
    diags.append(d)
    for at in (2, 4):
        state, d = pl.pallas_call(
            functools.partial(middle_kernel, at), out_shape=(full, dshape), scratch_shapes=[panel], cost_estimate=work
        )(state)
        diags.append(d)
    return pl.pallas_call(
        functools.partial(last_kernel, 6),
        out_shape=(half, half, half, half, jax.ShapeDtypeStruct((1, n), F32)),
        scratch_shapes=[pltpu.VMEM((n, n), F32), pltpu.VMEM((1, 2 * W), F32), pltpu.VMEM((n, n), F32), panel],
        cost_estimate=work,
        name="panels6",
    )(state, *diags)


def apply_inverse(x, high, low):
    h = high.shape[0] // 2
    xh, xl = split(x)
    first = dot3(xh[:, :h], xl[:, :h], high[:h, :h], low[:h, :h])
    second = dot3(xh, xl, high[:, h:], low[:, h:])
    return jnp.concatenate([first, second], axis=1)


def own_kernel(keep, x, high, low, diag, out):
    i = pl.program_id(0)
    y = apply_inverse(x[0], high, low) / diag[...]
    out[0] = jnp.where(keep[i] > 0, y, 0.0)


def own_factors(panel_rows, high, low, diag, usable):
    slots, b, n = panel_rows.shape
    const = lambda i, k: (0, 0)
    return pl.pallas_call(
        own_kernel,
        out_shape=jax.ShapeDtypeStruct(panel_rows.shape, F32),
        grid_spec=pltpu.PrefetchScalarGridSpec(
            num_scalar_prefetch=1,
            grid=(slots,),
            in_specs=[
                pl.BlockSpec((1, b, n), lambda i, k: (i, 0, 0)),
                pl.BlockSpec((n, n), const),
                pl.BlockSpec((n, n), const),
                pl.BlockSpec((1, n), const),
            ],
            out_specs=pl.BlockSpec((1, b, n), lambda i, k: (i, 0, 0)),
        ),
        cost_estimate=cost(slots * b * n * n * 6, slots * b * n * 8),
        name="own_factors",
    )(usable.astype(jnp.int32), panel_rows, high, low, diag)


def pick_kernel(place, *refs):
    nz, ny = 8, 4
    zy = refs[:nz]
    yz = refs[nz : nz + ny]
    outs = refs[nz + ny : nz + ny + 2]
    sems = refs[nz + ny + 2]
    count, rows, _ = outs[0].shape
    half = rows // 2

    def copy(color, which, g, source, at):
        target = outs[which].at[g, pl.ds(color * half, half)]
        return pltpu.make_async_copy(source.at[at], target, sems.at[color, which, g])

    for which in range(2):

        @pl.loop(0, count)
        def _(g):
            ez, ey, slot = place[which, 0, g], place[which, 1, g], place[which, 2, g]
            for e in range(nz):

                @pl.when(ez == e)
                def _():
                    copy(0, which, g, zy[e], ey * 2 + slot).start()

            for e in range(ny):

                @pl.when(ey == e)
                def _():
                    copy(1, which, g, yz[e], ez * 2 + slot).start()

    for which in range(2):

        @pl.loop(0, count)
        def _(g):
            copy(0, which, g, zy[0], 0).wait()
            copy(1, which, g, yz[0], 0).wait()


def pick(zy, yz, place, rows, n):
    count = place.shape[2]
    shape = jax.ShapeDtypeStruct((count, rows, n), F32)
    return pl.pallas_call(
        pick_kernel,
        out_shape=(shape, shape),
        grid_spec=pltpu.PrefetchScalarGridSpec(
            num_scalar_prefetch=1,
            grid=(),
            in_specs=[pl.BlockSpec(memory_space=pl.ANY)] * (len(zy) + len(yz)),
            out_specs=(pl.BlockSpec(memory_space=pltpu.VMEM),) * 2,
            scratch_shapes=[pltpu.SemaphoreType.DMA((2, 2, count))],
        ),
        cost_estimate=cost(0, 4 * 4 * count * rows * n),
        name="pick",
    )(place, *zy, *yz)


def update_kernel(info, tile, full_high, full_low, p0, p1, p2, p3, table, out, stage, lh, ll, rh, rl, sems):
    k = pl.program_id(0)
    count, b, _ = stage.shape
    half = count // 2
    rows = p0.shape[1]
    tail = table.shape[1]

    @pl.when(k == 0)
    def _():
        parts = [
            pltpu.make_async_copy(p, stage.at[:, pl.ds(pl.multiple_of(info[3, i] * rows, rows), rows), :], sems.at[count + i])
            for i, p in enumerate((p0, p1, p2, p3))
        ]
        for c in parts:
            c.start()

        def rest(g):
            return pltpu.make_async_copy(table.at[info[4, g]], stage.at[g, pl.ds(b - tail, tail), :], sems.at[g])

        @pl.loop(0, half)
        def _(g):
            rest(g).start()
            rest(g + half).start()

        for c in parts:
            c.wait()

        @pl.loop(0, half)
        def _(g):
            rest(g).wait()
            rest(g + half).wait()
            xh, xl = split(jnp.where(info[5, g] > 0, stage[g], 0.0))
            yh, yl = split(dot3(xh, xl, full_high[...], full_low[...]))
            lh[g] = yh
            ll[g] = yl
            xh, xl = split(jnp.where(info[5, g + half] > 0, stage[g + half], 0.0))
            rh[g] = xh
            rl[g] = xl

    @pl.loop(0, tile.shape[0], unroll=2)
    def _(t):
        slot = k * tile.shape[0] + t
        i, j = info[0, slot], info[1, slot]
        product = dot3(lh[i], ll[i], rh[j], rl[j], nt=True)
        out[t] = tile[t] - jnp.where(info[2, slot] > 0, product, 0.0)


def update_tiles(tiles, full_high, full_low, parts, quarters, table, slots, valid, pairs):
    total, b, _ = tiles.shape
    count = slots.shape[0]
    half = count // 2
    n = full_high.shape[0]
    widest = max(total, count)
    fit = lambda v: jnp.pad(v.astype(jnp.int32), (0, widest - v.shape[0]))
    info = jnp.stack(
        [
            fit(jnp.minimum(pairs[:, 0], half - 1)),
            fit(jnp.clip(pairs[:, 1] - half, 0, half - 1)),
            fit(pairs[:, 0] < count),
            fit(jnp.stack(quarters)),
            fit(slots),
            fit(valid),
        ]
    )
    block = 4 if total % 4 == 0 else 1
    tspec = pl.BlockSpec((block, b, b), lambda k, s: (k, 0, 0))
    whole = pl.BlockSpec((n, n), lambda k, s: (0, 0))
    anywhere = pl.BlockSpec(memory_space=pl.ANY)
    operand = pltpu.VMEM((half, b, n), BF)
    return pl.pallas_call(
        update_kernel,
        out_shape=jax.ShapeDtypeStruct(tiles.shape, F32),
        grid_spec=pltpu.PrefetchScalarGridSpec(
            num_scalar_prefetch=1,
            grid=(total // block,),
            in_specs=[tspec, whole, whole] + [anywhere] * 5,
            out_specs=tspec,
            scratch_shapes=[pltpu.VMEM((count, b, n), F32)]
            + [operand] * 4
            + [pltpu.SemaphoreType.DMA((count + 4,))],
        ),
        compiler_params=pltpu.CompilerParams(vmem_limit_bytes=58 * 2**20),
        cost_estimate=cost(total * b * b * n * 6 + half * b * n * n * 6, total * b * 8 * b + count * b * n * 4),
        name="update_tiles",
    )(info, tiles, full_high, full_low, *parts, table)


def turned(core, step):
    return step if core == 0 else -step


def tile_of(y, z, core):
    return ((y % NY) * NZ + z % NZ) * 2 + core


def chips():
    return [(y, z, c) for y in range(NY) for z in range(NZ) for c in range(2)]


def z_perm(step):
    return [(tile_of(y, z, c), tile_of(y, z + turned(c, step), c)) for y, z, c in chips()]


def y_perm(step):
    return [(tile_of(y, z, c), tile_of(y + turned(c, step), z, c)) for y, z, c in chips()]


def x_perm(tiles, reps, step):
    return [(t * reps + x, t * reps + (x + turned(t % 2, step)) % reps) for t in range(tiles) for x in range(reps)]


def ring(block, size, ahead, back):
    near, far = [block], [block]
    for k in range(size // 2):
        near.append(lax.ppermute(near[-1], "tiles", ahead))
        if k < size // 2 - 1:
            far.append(lax.ppermute(far[-1], "tiles", back))
    return near + far[:0:-1]


def per_device(tiles, reps, trailing_tiles, panel_rows, pivot_blocks, coupling, row_ids, membership, tile_pairs):
    owned_slots, b, n = panel_rows.shape
    tile_index = lax.axis_index("tiles")
    rep_index = lax.axis_index("rep")
    core, my_z, my_y = tile_index % 2, (tile_index // 2) % NZ, tile_index // (2 * NZ)
    turn = 1 - 2 * core
    own_ids = lax.dynamic_slice_in_dim(row_ids, tile_index * owned_slots, owned_slots)

    quarter = SPLIT // reps
    gathered = lax.all_gather(panel_rows[:, SPLIT:], "tiles", axis=0, tiled=True)
    half = quarter // 2
    top = lax.dynamic_slice_in_dim(panel_rows, rep_index * quarter, half, 1)
    low_rows = lax.dynamic_slice_in_dim(panel_rows, rep_index * quarter + half, half, 1)
    za, zb, ya, yb = z_perm(1), z_perm(-1), y_perm(1), y_perm(-1)
    zy = ring(jnp.concatenate(ring(top, NY, ya, yb), axis=0), NZ, za, zb)
    yz = ring(jnp.concatenate(ring(low_rows, NZ, za, zb), axis=0), NY, ya, yb)

    both_lists = lax.dynamic_slice_in_dim(membership, (tile_index // 2) * 2, 2, 0)
    match = both_lists[:, :, None] == row_ids[None, None, :]
    position = jnp.arange(row_ids.shape[0], dtype=jnp.int32)
    where = jnp.max(jnp.where(match, position[None, None, :], 0), axis=2)
    where = jnp.where(core == 0, where, where[::-1])
    slots = where[0]
    valid = (lax.dynamic_index_in_dim(membership, tile_index, 0, keepdims=False) < NB).astype(jnp.int32)
    ez = (turn * (my_z - (where // 4) % NZ)) % NZ
    ey = (turn * (my_y - where // (4 * NZ))) % NY
    place = jnp.stack([ez, ey, where % owned_slots], axis=1)
    here = (slots // 2) % 2 == core

    mine, theirs = pick(zy, yz, place, quarter, n)
    swap = [(t, t ^ 1) for t in range(tiles)]
    mine = jnp.where(here[:, None, None], mine, lax.ppermute(theirs, "tiles", swap))
    both = ("tiles", "rep")
    ahead, back = x_perm(tiles, reps, 1), x_perm(tiles, reps, -1)
    one = lax.ppermute(mine, both, ahead)
    other = lax.ppermute(mine, both, back)
    far = lax.ppermute(one, both, ahead)
    quarters = [(rep_index + shift + reps) % reps for shift in (0, -turn, turn, 2)]

    high, low, full_high, full_low, diag = factorize(pivot_blocks, coupling)
    factors = own_factors(panel_rows, high, low, diag, own_ids < NB)
    parts = (mine, one, other, far)
    updated = update_tiles(trailing_tiles, full_high, full_low, parts, quarters, gathered, slots, valid, tile_pairs)
    return (updated, factors, diag.reshape(2, b))


def solution(mesh):
    return jax.shard_map(
        functools.partial(per_device, mesh.shape["tiles"], mesh.shape["rep"]),
        mesh=mesh,
        in_specs=(
            P(("tiles", "rep"), None, None),
            P("tiles", None, None),
            P(),
            P(),
            P(),
            P(),
            P(("tiles", "rep"), None),
        ),
        out_specs=(P(("tiles", "rep"), None, None), P("tiles", None, None), P()),
        check_vma=False,
    )
```

```python
import functools

import jax
import jax.numpy as jnp
from jax import lax
from jax.experimental import pallas as pl
from jax.experimental.pallas import tpu as pltpu
from jax.sharding import PartitionSpec as P


NB = 96
NY, NZ = 4, 8
SPLIT = 128
W = 64
GROUP = 4
F32 = jnp.float32
BF = jnp.bfloat16
HI = lax.Precision.HIGHEST


def dot(a, b):
    return lax.dot_general(a, b, (((1,), (0,)), ((), ())), precision=HI, preferred_element_type=F32)


def dot_nt(a, b):
    return lax.dot_general(a, b, (((1,), (1,)), ((), ())), precision=HI, preferred_element_type=F32)


def split(x):
    hi = x.astype(BF)
    return hi, (x - hi.astype(F32)).astype(BF)


def dot3(ah, al, bh, bl, nt=False):
    dims = (((1,), (1 if nt else 0,)), ((), ()))
    f = functools.partial(lax.dot_general, dimension_numbers=dims, preferred_element_type=F32)
    return f(ah, bh) + (f(ah, bl) + f(al, bh))


def load_panel(state, work, at):
    lo, up = at * W, (at + 1) * W
    eye = lax.broadcasted_iota(jnp.int32, (W, W), 0) == lax.broadcasted_iota(jnp.int32, (W, W), 1)
    work[...] = jnp.concatenate([state[lo:up, lo:up], eye.astype(F32)], axis=1)


def pivot_steps(work):
    rows = lax.broadcasted_iota(jnp.int32, (W, 2 * W), 0)
    aug = work[...]
    for first in range(0, W, GROUP):
        columns = [jnp.broadcast_to(aug[:, k : k + 1], (W, 2 * W)) for k in range(first, first + GROUP)]
        for k in range(first, first + GROUP):
            column = columns[k - first]
            reciprocal = 1.0 / column[k : k + 1, :]
            below = jnp.where(rows > k, column, 0.0)
            aug = aug - below * (aug[k : k + 1, :] * reciprocal)
            for later in range(k + 1 - first, GROUP):
                columns[later] = columns[later] - below * (columns[later][k : k + 1, :] * reciprocal)
    work[...] = aug


def finish_panel(state, work, diag, at, n):
    lo, up = at * W, (at + 1) * W
    rows = lax.broadcasted_iota(jnp.int32, (W, 2 * W), 0)
    lanes = lax.broadcasted_iota(jnp.int32, (W, 2 * W), 1)
    aug = work[...]
    inverse = aug[:, W:]
    on_diag = jnp.where(rows == lanes, aug, 0.0)
    d_col = jnp.sum(on_diag, axis=1, keepdims=True)
    diag[0:1, (at % 2) * W : (at % 2 + 1) * W] = jnp.sum(on_diag, axis=0, keepdims=True)[:, :W]
    width = state.shape[1]
    col = lax.broadcasted_iota(jnp.int32, (W, width), 1)
    row = lax.broadcasted_iota(jnp.int32, (W, width), 0)
    own = jnp.where((col >= lo) & (col < up), (col - lo == row).astype(F32), state[lo:up, :])
    if up < n:
        below = dot(dot_nt(state[up:n, lo:up], inverse), inverse / d_col)
        base = state[up:n, :]
        bcol = lax.broadcasted_iota(jnp.int32, base.shape, 1)
        base = jnp.where((bcol >= lo) & (bcol < up), 0.0, base)
        state[up:n, :] = base - dot(below, own)
    state[lo:up, :] = jnp.where(col < up, dot(inverse, own), 0.0)


def eliminate(state, diag, work, at):
    @pl.loop(0, 2)
    def _(i):
        for p in range(2):

            @pl.when(i == p)
            def _():
                load_panel(state, work, at + p)

        pivot_steps(work)
        for p in range(2):

            @pl.when(i == p)
            def _():
                finish_panel(state, work, diag, at + p, state.shape[0])


def first_kernel(pivot, coupling, state, diag, work):
    h = coupling.shape[0]
    state[:h, :h] = pivot[0]
    state[h:, :h] = coupling[...]
    state[:h, h:] = coupling[...].T
    state[h:, h:] = pivot[1]
    eliminate(state, diag, work, 0)


def middle_kernel(at, before, state, diag, work):
    state[...] = before[...]
    eliminate(state, diag, work, at)


def last_kernel(at, before, d0, d1, d2, high, low, full_high, full_low, diag, state, last, scaled, work):
    state[...] = before[...]
    eliminate(state, last, work, at)
    for p, d in enumerate((d0, d1, d2, last)):
        diag[0:1, p * 2 * W : (p + 1) * 2 * W] = d[...]
    turned = state[...].T
    high[...], low[...] = split(turned)
    scaled[...] = turned / diag[...]
    step = 2 * W

    @pl.loop(0, state.shape[0] // step)
    def _(i):
        at = pl.ds(pl.multiple_of(i * step, step), step)
        full_high[at, :], full_low[at, :] = split(dot(scaled[at, :], state[...]))


def cost(flops, nbytes):
    return pl.CostEstimate(flops=int(flops), bytes_accessed=int(nbytes), transcendentals=0)


def factorize(pivot_blocks, coupling):
    n = 2 * coupling.shape[0]
    full = jax.ShapeDtypeStruct((n, n), F32)
    half = jax.ShapeDtypeStruct((n, n), BF)
    dshape = jax.ShapeDtypeStruct((1, 2 * W), F32)
    work = cost(6e9, 2 * n * n * 4)
    diags = []
    panel = pltpu.VMEM((W, 2 * W), F32)
    state, d = pl.pallas_call(
        first_kernel, out_shape=(full, dshape), scratch_shapes=[panel], cost_estimate=work, name="panels0"
    )(pivot_blocks, coupling)
    diags.append(d)
    for at in (2, 4):
        state, d = pl.pallas_call(
            functools.partial(middle_kernel, at), out_shape=(full, dshape), scratch_shapes=[panel], cost_estimate=work
        )(state)
        diags.append(d)
    return pl.pallas_call(
        functools.partial(last_kernel, 6),
        out_shape=(half, half, half, half, jax.ShapeDtypeStruct((1, n), F32)),
        scratch_shapes=[pltpu.VMEM((n, n), F32), pltpu.VMEM((1, 2 * W), F32), pltpu.VMEM((n, n), F32), panel],
        cost_estimate=work,
        name="panels6",
    )(state, *diags)


def apply_inverse(x, high, low):
    h = high.shape[0] // 2
    xh, xl = split(x)
    first = dot3(xh[:, :h], xl[:, :h], high[:h, :h], low[:h, :h])
    second = dot3(xh, xl, high[:, h:], low[:, h:])
    return jnp.concatenate([first, second], axis=1)


def own_kernel(keep, x, high, low, diag, out):
    i = pl.program_id(0)
    y = apply_inverse(x[0], high, low) / diag[...]
    out[0] = jnp.where(keep[i] > 0, y, 0.0)


def own_factors(panel_rows, high, low, diag, usable):
    slots, b, n = panel_rows.shape
    const = lambda i, k: (0, 0)
    return pl.pallas_call(
        own_kernel,
        out_shape=jax.ShapeDtypeStruct(panel_rows.shape, F32),
        grid_spec=pltpu.PrefetchScalarGridSpec(
            num_scalar_prefetch=1,
            grid=(slots,),
            in_specs=[
                pl.BlockSpec((1, b, n), lambda i, k: (i, 0, 0)),
                pl.BlockSpec((n, n), const),
                pl.BlockSpec((n, n), const),
                pl.BlockSpec((1, n), const),
            ],
            out_specs=pl.BlockSpec((1, b, n), lambda i, k: (i, 0, 0)),
        ),
        cost_estimate=cost(slots * b * n * n * 6, slots * b * n * 8),
        name="own_factors",
    )(usable.astype(jnp.int32), panel_rows, high, low, diag)


def pick_kernel(place, *refs):
    nz, ny = 8, 4
    zy = refs[:nz]
    yz = refs[nz : nz + ny]
    outs = refs[nz + ny : nz + ny + 2]
    sems = refs[nz + ny + 2]
    count, rows, _ = outs[0].shape
    half = rows // 2

    def copy(color, which, g, source, at):
        target = outs[which].at[g, pl.ds(color * half, half)]
        return pltpu.make_async_copy(source.at[at], target, sems.at[color, which, g])

    for which in range(2):

        @pl.loop(0, count)
        def _(g):
            ez, ey, slot = place[which, 0, g], place[which, 1, g], place[which, 2, g]
            for e in range(nz):

                @pl.when(ez == e)
                def _():
                    copy(0, which, g, zy[e], ey * 2 + slot).start()

            for e in range(ny):

                @pl.when(ey == e)
                def _():
                    copy(1, which, g, yz[e], ez * 2 + slot).start()

    for which in range(2):

        @pl.loop(0, count)
        def _(g):
            copy(0, which, g, zy[0], 0).wait()
            copy(1, which, g, yz[0], 0).wait()


def pick(zy, yz, place, rows, n):
    count = place.shape[2]
    shape = jax.ShapeDtypeStruct((count, rows, n), F32)
    return pl.pallas_call(
        pick_kernel,
        out_shape=(shape, shape),
        grid_spec=pltpu.PrefetchScalarGridSpec(
            num_scalar_prefetch=1,
            grid=(),
            in_specs=[pl.BlockSpec(memory_space=pl.ANY)] * (len(zy) + len(yz)),
            out_specs=(pl.BlockSpec(memory_space=pltpu.VMEM),) * 2,
            scratch_shapes=[pltpu.SemaphoreType.DMA((2, 2, count))],
        ),
        cost_estimate=cost(0, 4 * 4 * count * rows * n),
        name="pick",
    )(place, *zy, *yz)


def left_kernel(info, p0, p1, p2, p3, full_high, full_low, high, low):
    step, rows, _ = p0.shape
    first = pl.program_id(0) * step
    parts = (p0, p1, p2, p3)
    pieces = [jnp.where(info[4 + first + g] > 0, p[g], 0.0) for p in parts for g in range(step)]
    xh, xl = split(jnp.concatenate(pieces, axis=0))
    yh, yl = split(dot3(xh, xl, full_high[...], full_low[...]))
    for i in range(len(parts)):
        at = pl.ds(pl.multiple_of(info[i] * rows, rows), rows)
        for g in range(step):
            here = slice((i * step + g) * rows, (i * step + g + 1) * rows)
            high[g, at, :] = yh[here]
            low[g, at, :] = yl[here]


def left_rows(parts, full_high, full_low, quarters, valid):
    count, rows, n = parts[0].shape
    half = count // 2
    step = 2
    head = rows * len(parts)
    info = jnp.concatenate([jnp.stack(quarters), valid[:half]]).astype(jnp.int32)
    shape = jax.ShapeDtypeStruct((half, head, n), BF)
    whole = pl.BlockSpec((n, n), lambda i, s: (0, 0))
    target = pl.BlockSpec((step, head, n), lambda i, s: (i, 0, 0))
    return pl.pallas_call(
        left_kernel,
        out_shape=(shape, shape),
        grid_spec=pltpu.PrefetchScalarGridSpec(
            num_scalar_prefetch=1,
            grid=(half // step,),
            in_specs=[pl.BlockSpec((step, rows, n), lambda i, s: (i, 0, 0))] * len(parts) + [whole, whole],
            out_specs=(target, target),
        ),
        cost_estimate=cost(half * head * n * n * 6, half * head * n * 8),
        name="left_rows",
    )(info, *parts, full_high, full_low)


def update_kernel(info, tile, full_high, full_low, gh, gl, p0, p1, p2, p3, table, out, near, side, lh, ll, rh, rl, sems):
    k = pl.program_id(0)
    half, b, _ = side.shape
    tail = near.shape[1]
    head = b - tail
    rows = p0.shape[1]

    @pl.when(k == 0)
    def _():
        parts = [
            pltpu.make_async_copy(
                p.at[pl.ds(half, half)],
                side.at[:, pl.ds(pl.multiple_of(info[3, i] * rows, rows), rows), :],
                sems.at[2 * half + i],
            )
            for i, p in enumerate((p0, p1, p2, p3))
        ]
        ready = [
            pltpu.make_async_copy(gh, lh.at[:, pl.ds(0, head), :], sems.at[2 * half + 4]),
            pltpu.make_async_copy(gl, ll.at[:, pl.ds(0, head), :], sems.at[2 * half + 5]),
        ]

        def rest(g):
            return (
                pltpu.make_async_copy(table.at[info[4, g]], near.at[g], sems.at[g]),
                pltpu.make_async_copy(table.at[info[4, half + g]], side.at[g, pl.ds(head, tail), :], sems.at[half + g]),
            )

        for c in parts:
            c.start()

        @pl.loop(0, half)
        def _(g):
            for c in rest(g):
                c.start()

        for c in ready:
            c.start()
        for c in parts:
            c.wait()

        @pl.loop(0, half // 2)
        def _(i):
            pair = (2 * i, 2 * i + 1)
            for g in pair:
                for c in rest(g):
                    c.wait()
            xh, xl = split(jnp.concatenate([jnp.where(info[5, g] > 0, near[g], 0.0) for g in pair], axis=0))
            yh, yl = split(dot3(xh, xl, full_high[...], full_low[...]))
            for at, g in enumerate(pair):
                lh[g, pl.ds(head, tail), :] = yh[at * tail : (at + 1) * tail]
                ll[g, pl.ds(head, tail), :] = yl[at * tail : (at + 1) * tail]
                xh, xl = split(jnp.where(info[5, half + g] > 0, side[g], 0.0))
                rh[g] = xh
                rl[g] = xl

        for c in ready:
            c.wait()

    @pl.loop(0, tile.shape[0], unroll=2)
    def _(t):
        slot = k * tile.shape[0] + t
        i, j = info[0, slot], info[1, slot]
        product = dot3(lh[i], ll[i], rh[j], rl[j], nt=True)
        out[t] = tile[t] - jnp.where(info[2, slot] > 0, product, 0.0)


def update_tiles(tiles, full_high, full_low, left, parts, quarters, table, slots, valid, pairs):
    total, b, _ = tiles.shape
    count = slots.shape[0]
    half = count // 2
    n = full_high.shape[0]
    widest = max(total, count)
    fit = lambda v: jnp.pad(v.astype(jnp.int32), (0, widest - v.shape[0]))
    info = jnp.stack(
        [
            fit(jnp.minimum(pairs[:, 0], half - 1)),
            fit(jnp.clip(pairs[:, 1] - half, 0, half - 1)),
            fit(pairs[:, 0] < count),
            fit(jnp.stack(quarters)),
            fit(slots),
            fit(valid),
        ]
    )
    block = 4 if total % 4 == 0 else 1
    tspec = pl.BlockSpec((block, b, b), lambda k, s: (k, 0, 0))
    whole = pl.BlockSpec((n, n), lambda k, s: (0, 0))
    anywhere = pl.BlockSpec(memory_space=pl.ANY)
    operand = pltpu.VMEM((half, b, n), BF)
    return pl.pallas_call(
        update_kernel,
        out_shape=jax.ShapeDtypeStruct(tiles.shape, F32),
        grid_spec=pltpu.PrefetchScalarGridSpec(
            num_scalar_prefetch=1,
            grid=(total // block,),
            in_specs=[tspec, whole, whole] + [anywhere] * 7,
            out_specs=tspec,
            scratch_shapes=[pltpu.VMEM((half, table.shape[1], n), F32), pltpu.VMEM((half, b, n), F32)]
            + [operand] * 4
            + [pltpu.SemaphoreType.DMA((count + 6,))],
        ),
        compiler_params=pltpu.CompilerParams(vmem_limit_bytes=58 * 2**20),
        cost_estimate=cost(total * b * b * n * 6 + half * b * n * n * 6, total * b * 8 * b + count * b * n * 4),
        name="update_tiles",
    )(info, tiles, full_high, full_low, *left, *parts, table)


def turned(core, step):
    return step if core == 0 else -step


def tile_of(y, z, core):
    return ((y % NY) * NZ + z % NZ) * 2 + core


def chips():
    return [(y, z, c) for y in range(NY) for z in range(NZ) for c in range(2)]


def z_perm(step):
    return [(tile_of(y, z, c), tile_of(y, z + turned(c, step), c)) for y, z, c in chips()]


def y_perm(step):
    return [(tile_of(y, z, c), tile_of(y + turned(c, step), z, c)) for y, z, c in chips()]


def x_perm(tiles, reps, step):
    return [(t * reps + x, t * reps + (x + turned(t % 2, step)) % reps) for t in range(tiles) for x in range(reps)]


def ring(block, size, ahead, back):
    near, far = [block], [block]
    for k in range(size // 2):
        near.append(lax.ppermute(near[-1], "tiles", ahead))
        if k < size // 2 - 1:
            far.append(lax.ppermute(far[-1], "tiles", back))
    return near + far[:0:-1]


def per_device(tiles, reps, trailing_tiles, panel_rows, pivot_blocks, coupling, row_ids, membership, tile_pairs):
    owned_slots, b, n = panel_rows.shape
    tile_index = lax.axis_index("tiles")
    rep_index = lax.axis_index("rep")
    core, my_z, my_y = tile_index % 2, (tile_index // 2) % NZ, tile_index // (2 * NZ)
    turn = 1 - 2 * core
    own_ids = lax.dynamic_slice_in_dim(row_ids, tile_index * owned_slots, owned_slots)

    quarter = SPLIT // reps
    gathered = lax.all_gather(panel_rows[:, SPLIT:], "tiles", axis=0, tiled=True)
    half = quarter // 2
    top = lax.dynamic_slice_in_dim(panel_rows, rep_index * quarter, half, 1)
    low_rows = lax.dynamic_slice_in_dim(panel_rows, rep_index * quarter + half, half, 1)
    za, zb, ya, yb = z_perm(1), z_perm(-1), y_perm(1), y_perm(-1)
    zy = ring(jnp.concatenate(ring(top, NY, ya, yb), axis=0), NZ, za, zb)
    yz = ring(jnp.concatenate(ring(low_rows, NZ, za, zb), axis=0), NY, ya, yb)

    both_lists = lax.dynamic_slice_in_dim(membership, (tile_index // 2) * 2, 2, 0)
    match = both_lists[:, :, None] == row_ids[None, None, :]
    position = jnp.arange(row_ids.shape[0], dtype=jnp.int32)
    where = jnp.max(jnp.where(match, position[None, None, :], 0), axis=2)
    where = jnp.where(core == 0, where, where[::-1])
    slots = where[0]
    valid = (lax.dynamic_index_in_dim(membership, tile_index, 0, keepdims=False) < NB).astype(jnp.int32)
    ez = (turn * (my_z - (where // 4) % NZ)) % NZ
    ey = (turn * (my_y - where // (4 * NZ))) % NY
    place = jnp.stack([ez, ey, where % owned_slots], axis=1)
    here = (slots // 2) % 2 == core

    mine, theirs = pick(zy, yz, place, quarter, n)
    swap = [(t, t ^ 1) for t in range(tiles)]
    mine = jnp.where(here[:, None, None], mine, lax.ppermute(theirs, "tiles", swap))
    both = ("tiles", "rep")
    ahead, back = x_perm(tiles, reps, 1), x_perm(tiles, reps, -1)
    one = lax.ppermute(mine, both, ahead)
    other = lax.ppermute(mine, both, back)
    far = lax.ppermute(one, both, ahead)
    quarters = [(rep_index + shift + reps) % reps for shift in (0, -turn, turn, 2)]

    high, low, full_high, full_low, diag = factorize(pivot_blocks, coupling)
    factors = own_factors(panel_rows, high, low, diag, own_ids < NB)
    parts = (mine, one, other, far)
    left = left_rows(parts, full_high, full_low, quarters, valid)
    updated = update_tiles(trailing_tiles, full_high, full_low, left, parts, quarters, gathered, slots, valid, tile_pairs)
    return (updated, factors, diag.reshape(2, b))


def solution(mesh):
    return jax.shard_map(
        functools.partial(per_device, mesh.shape["tiles"], mesh.shape["rep"]),
        mesh=mesh,
        in_specs=(
            P(("tiles", "rep"), None, None),
            P("tiles", None, None),
            P(),
            P(),
            P(),
            P(),
            P(("tiles", "rep"), None),
        ),
        out_specs=(P(("tiles", "rep"), None, None), P("tiles", None, None), P()),
        check_vma=False,
    )
```
